128 devices in a mesh: freq: 8 (over x_hi, z), cell: 16 (over x_lo, y, core).
Axes of the slice: x: 4 (x_hi: 2, x_lo: 2; x = x_hi * 2 + x_lo), y: 4, z: 4, core: 2. Of those that a mesh axis runs over, the one named last changes fastest.
Arguments:
- green: bfloat16 [2, 16, 1024, 8192], P(None, 'freq', None, 'cell'), may hold values from -0.25 to 0.25
- coeffs: float32 [8, 8192], P('freq', 'cell'), may hold values from -6 to 6
- basis: float32 [16, 8], P('freq'), may hold values from -2 to 2
- amplitude: float32 [16, 1024], P('freq'), may hold values from 0.5 to 2
- block_mask: int32 [16, 16], replicated, may hold values 0 or 1
Outputs:
- hess_vec: float32 [8, 8192], P('freq', 'cell')
The draws below stay inside these ranges and needn't reach their ends.
All inputs are finite; a program needn't handle non-finite values.
Results may differ from the reference program's by a relative error of at most 0.0024.
Values may be sent and summed in bfloat16 or wider, within the bound.
A program may use at most 192 MiB of HBM per device.

```python
import math
import jax
import jax.numpy as jnp
from jax import lax

NS = 1024
SB = 64
NB = 8
CELL_DEV = 512
NF = 16
NC = 8192
NSB = 16
N_CELL = 16


def place_ends(result, key, low, largest):
    longest = result.shape.index(max(result.shape))
    spots = []
    for shift in (0, 1):
        where = [jax.random.randint(jax.random.fold_in(key, axis), (), 0, length) for axis, length in enumerate(result.shape)]
        where[longest] = (where[longest] + shift) % result.shape[longest]
        spots.append(tuple(where))
    return result.at[spots[0]].set(low).at[spots[1]].set(largest)


def raised(drawn, rng, source, target, shards_of, factor):
    owner, partner = [(jnp.arange(drawn.shape[dim]) // (drawn.shape[dim] // shards_of)).reshape([-1 if axis == dim else 1 for axis in range(drawn.ndim)]) for dim in (source, target)]
    chosen = jax.random.permutation(rng, shards_of)[partner]
    strong = (owner == chosen) | (owner == (partner + shards_of // 2) % shards_of)
    return jnp.where(strong, factor * drawn, drawn)


def level_of(stream_key, shape, pieces, least, high):
    def one(position, blocks):
        draws = jax.random.uniform(jax.random.fold_in(jax.random.fold_in(stream_key, 6), position), (blocks,), jnp.float32, least / len(pieces), high / len(pieces))
        return jnp.repeat(jnp.exp(draws), shape[position] // blocks).reshape((-1,) + (1,) * (len(shape) - position - 1))

    loudness = one(*pieces[0])
    for cut in pieces[1:]:
        loudness = loudness * one(*cut)
    return loudness


def scatter_about(rng, extent, scale, reach, pieces=(), held_as=jnp.bfloat16):
    level = level_of(rng, extent, pieces, -0.22, 0.18) if pieces else 1.0
    result = jax.random.normal(rng, extent, jnp.float32) * scale * level
    return jnp.minimum(jnp.maximum(result, -reach), reach).astype(held_as)


def bell_draw_with(own_key, shape, spread, limit, shards, heavy, held_as=jnp.bfloat16):
    entries = spread * jax.random.normal(own_key, shape, jnp.float32)
    if shards:
        entries = entries * level_of(own_key, shape, shards, -0.22, 0.18)
    return jnp.clip(raised(entries, jax.random.fold_in(own_key, 3), *heavy), -limit, limit).astype(held_as)


def setup_inputs(seed: int = 0) -> dict:
    key_list = jax.random.split(jax.random.key(seed), 6)
    return {
        "green": bell_draw_with(key_list[0], (2, NF, NS, NC), NS ** -0.5, 0.25, ((1, 8), (3, 16)), (3, 2, 16, 2.0)),
        "coeffs": scatter_about(key_list[1], (NB, NC), 1.0, 6.0, ((0, 8), (1, 16)), jnp.float32),
        "basis": scatter_about(key_list[2], (NF, NB), NB ** -0.5, 2.0, ((0, 8),), jnp.float32),
        "amplitude": jnp.clip(jnp.exp(math.log(2.0) - 1.3862944 * jax.random.uniform(key_list[3], (NF, NS), jnp.float32) ** level_of(key_list[3], (NF, NS), ((0, 8),), -0.2, 0.2)), 0.5, 2.0),
        "block_mask": place_ends((jax.random.randint(key_list[4], (NSB, NSB), 0, 4) < 3).astype(jnp.int32), jax.random.fold_in(key_list[4], 1), 0, 1),
    }


def reference(green, coeffs, basis, amplitude, block_mask):
    highest = lax.Precision.HIGHEST
    source = jnp.dot(basis, coeffs, precision=highest)
    scaled = (green.astype(jnp.float32) * source[None, :, None, :]).astype(jnp.bfloat16)

    def one_block(total, index):
        start = (index * CELL_DEV).astype(jnp.int32)
        left = lax.dynamic_slice_in_dim(scaled, start, CELL_DEV, 3).astype(jnp.float32)
        local = lax.dynamic_slice_in_dim(green, start, CELL_DEV, 3).astype(jnp.float32)
        right = jnp.stack((jnp.stack((local[0], local[1])), jnp.stack((-local[1], local[0]))))
        term = jnp.einsum("pfic,qpfjc->fqij", left, right)
        rounded = lax.optimization_barrier(term.astype(jnp.bfloat16))
        return total + rounded.astype(jnp.float32), None

    empty = jnp.zeros((NF, 2, NS, NS), jnp.float32)
    corr, _ = lax.scan(one_block, empty, jnp.arange(N_CELL, dtype=jnp.int32))
    expanded = jnp.broadcast_to(block_mask[:, None, :, None], (NSB, SB, NSB, SB)).reshape(NS, NS).astype(jnp.float32)
    weight = amplitude[:, :, None] * amplitude[:, None, :] * expanded[None]
    resid = (weight[:, None] * corr).astype(jnp.bfloat16)

    def sense(pair):
        rows, field = pair
        rf = rows.astype(jnp.float32)
        gf = field.astype(jnp.float32)
        yre = jnp.dot(rf[0], gf[0], preferred_element_type=jnp.float32) - jnp.dot(rf[1], gf[1], preferred_element_type=jnp.float32)
        yim = jnp.dot(rf[0], gf[1], preferred_element_type=jnp.float32) + jnp.dot(rf[1], gf[0], preferred_element_type=jnp.float32)
        return jnp.sum(gf[0] * yre + gf[1] * yim, axis=0)

    sens = lax.map(sense, (resid, jnp.moveaxis(green, 1, 0)))
    return jnp.dot(basis.T, sens, precision=highest)
```

```python
import functools

import jax
import jax.numpy as jnp
from jax import lax
from jax.experimental import pallas as pl
from jax.experimental.pallas import tpu as pltpu
from jax.sharding import PartitionSpec as P

MESH = pl.DeviceIdType.MESH
F32, BF16 = jnp.float32, jnp.bfloat16
NS = 1024
WAVES = 4
ROWS = NS // WAVES
UNIT = ROWS // 8
BLOCKS = 16
WIDTH = NS // BLOCKS


def dot_nt(a, b):
    return lax.dot_general(a, b, (((1,), (1,)), ((), ())), preferred_element_type=F32)


def dot_nn(a, b):
    return lax.dot_general(a, b, (((1,), (0,)), ((), ())), preferred_element_type=F32)


def kernel(
    nfreq,
    green,
    coeffs,
    basis,
    amp,
    mask,
    out,
    g,
    cbuf,
    sc,
    part,
    m1,
    m2,
    m3,
    relay,
    xsend,
    xrecv,
    keep,
    resid,
    weight,
    sens,
    fsend,
    frecv,
    own_sem,
    swap_send,
    swap_recv,
    c_send,
    c_recv,
    rs_send,
    rs_recv,
    ag_send,
    ag_recv,
    f_send,
    f_recv,
):
    q = lax.axis_index("freq")
    cell = lax.axis_index("cell")
    core = lax.rem(cell, 2)
    y = lax.rem(lax.div(cell, 2), 4)
    x = lax.div(cell, 8)
    yp, ym, y2 = lax.rem(y + 1, 4), lax.rem(y + 3, 4), lax.rem(y + 2, 4)

    def at(x_, y_, core_):
        return {"freq": q, "cell": x_ * 8 + y_ * 2 + core_}

    up, down = at(x, yp, core), at(x, ym, core)
    across, twin = at(1 - x, y, core), at(x, y, 1 - core)

    peers = [(d, h) for d in range(nfreq) for h in range(2) if (d, h) != (0, 0)]

    def peer(d, h):
        to_core = core if h == 0 else 1 - core
        to_q = lax.rem(q + d, nfreq)
        return {"freq": to_q, "cell": x * 8 + y * 2 + to_core}

    def remote(src, dst, send, recv, device):
        return pltpu.make_async_remote_copy(
            src_ref=src,
            dst_ref=dst,
            send_sem=send,
            recv_sem=recv,
            device_id=device,
            device_id_type=MESH,
        )

    own = [pltpu.make_async_copy(green.at[p, core], g.at[0, p], own_sem.at[p]) for p in range(2)]
    for copy in own:
        copy.start()

    barrier = pltpu.get_barrier_semaphore()
    met = [peer(d, h) for d, h in peers] + [up, down, across]
    for device in met:
        pl.semaphore_signal(barrier, inc=1, device_id=device, device_id_type=MESH)

    lane = lax.broadcasted_iota(jnp.int32, (1, NS), 1)
    block_of = lane // WIDTH
    amp_row = amp[pl.ds(core, 1), :]
    for w in range(WAVES):
        first = w * ROWS + (y * 2 + x) * UNIT
        a = lax.div(first, WIDTH)
        pair = jnp.zeros((1, NS), F32)
        for b in range(BLOCKS):
            m = (mask[a, b] + mask[b, a]).astype(F32)
            pair = pair + jnp.where(block_of == b, m, 0.0)
        row = lax.broadcasted_iota(jnp.int32, (UNIT, NS), 0) + first
        col = lax.broadcasted_iota(jnp.int32, (UNIT, NS), 1)
        same = row == col
        amp_col = jnp.sum(jnp.where(same, amp_row, 0.0), axis=1, keepdims=True)
        weight[w] = jnp.where(same, 0.5, 1.0) * (amp_col * (amp_row * pair))

    pl.semaphore_wait(barrier, len(met))

    c_copies = []
    for n, (d, h) in enumerate(peers):
        c_copies.append(
            remote(coeffs, cbuf.at[q, h], c_send.at[n], c_recv.at[n], peer(d, h))
        )
        c_copies[-1].start()
    swap = [
        remote(green.at[p, 1 - core], g.at[1, p], swap_send.at[p], swap_recv.at[p], twin)
        for p in range(2)
    ]
    for copy in swap:
        copy.start()
    cbuf[q, 0] = coeffs[...]

    for copy in c_copies:
        copy.wait_recv()
    source = []
    for h in range(2):
        total = basis[core, 0] * cbuf[0, h]
        for b in range(1, nfreq):
            total = total + basis[core, b] * cbuf[b, h]
        source.append(total)

    for copy in own:
        copy.wait()
    for copy in swap:
        copy.wait_recv()

    sent = []

    def start(copy):
        copy.start()
        sent.append(copy)

    def rs_up(w, n, src, dst):
        return remote(src, dst, rs_send.at[w, n, 0], rs_recv.at[w, n, 0], up)

    def rs_down(w, n, src, dst):
        return remote(src, dst, rs_send.at[w, n, 1], rs_recv.at[w, n, 1], down)

    def ag(w, n, unit, device):
        ref = resid.at[w, unit]
        return remote(ref, ref, ag_send.at[w, n], ag_recv.at[w, unit], device)

    def produce(w):
        rows = pl.ds(w * ROWS, ROWS)
        for h in range(2):
            for p in range(2):
                sc[h, p] = (g[h, p, rows, :].astype(F32) * source[h]).astype(BF16)

        def real(j):
            cols = pl.ds(j * ROWS, ROWS)
            total = dot_nt(sc[0, 0], g[0, 0, cols, :])
            total += dot_nt(sc[0, 1], g[0, 1, cols, :])
            total += dot_nt(sc[1, 0], g[1, 0, cols, :])
            total += dot_nt(sc[1, 1], g[1, 1, cols, :])
            return total

        def imag(j):
            cols = pl.ds(j * ROWS, ROWS)
            plus = dot_nt(sc[0, 1], g[0, 0, cols, :])
            plus += dot_nt(sc[1, 1], g[1, 0, cols, :])
            minus = dot_nt(sc[0, 0], g[0, 1, cols, :])
            minus += dot_nt(sc[1, 0], g[1, 1, cols, :])
            return plus - minus

        def put(j, block):
            part[w, :, :, pl.ds(j * ROWS, ROWS)] = block.astype(BF16).reshape(8, UNIT, ROWS)

        for j in range(w):
            put(j, imag(j))
        i_ = lax.broadcasted_iota(jnp.int32, (ROWS, ROWS), 0)
        j_ = lax.broadcasted_iota(jnp.int32, (ROWS, ROWS), 1)
        put(w, jnp.where(i_ <= j_, real(w), imag(w)))
        for j in range(w + 1, WAVES):
            put(j, real(j))
        start(rs_up(w, 0, part.at[w, y2 * 2], m1.at[w, 0]))
        start(rs_down(w, 0, part.at[w, y2 * 2 + 1], m1.at[w, 1]))
        start(rs_up(w, 1, part.at[w, yp * 2 + 1], m2.at[w, 0]))
        start(rs_down(w, 1, part.at[w, ym * 2], m2.at[w, 1]))

    def pass_on(w):
        rs_up(w, 0, part.at[w, y2 * 2], m1.at[w, 0]).wait_recv()
        relay[w, 0] = (part[w, yp * 2].astype(F32) + m1[w, 0].astype(F32)).astype(BF16)
        start(rs_up(w, 2, relay.at[w, 0], m3.at[w, 0]))
        rs_down(w, 0, part.at[w, y2 * 2 + 1], m1.at[w, 1]).wait_recv()
        relay[w, 1] = (part[w, ym * 2 + 1].astype(F32) + m1[w, 1].astype(F32)).astype(BF16)
        start(rs_down(w, 2, relay.at[w, 1], m3.at[w, 1]))

    def cross(w):
        return remote(xsend.at[w], xrecv.at[w], rs_send.at[w, 3, 0], rs_recv.at[w, 3, 0], across)

    def collect(w):
        rs_up(w, 1, part.at[w, yp * 2 + 1], m2.at[w, 0]).wait_recv()
        rs_down(w, 1, part.at[w, ym * 2], m2.at[w, 1]).wait_recv()
        rs_up(w, 2, relay.at[w, 0], m3.at[w, 0]).wait_recv()
        rs_down(w, 2, relay.at[w, 1], m3.at[w, 1]).wait_recv()
        low = part[w, y * 2].astype(F32) + m3[w, 0].astype(F32) + m2[w, 1].astype(F32)
        high = part[w, y * 2 + 1].astype(F32) + m3[w, 1].astype(F32) + m2[w, 0].astype(F32)
        mine = x == 0
        xsend[w] = jnp.where(mine, high, low).astype(BF16)
        start(cross(w))
        keep[w] = jnp.where(mine, low, high)

    def finish(w):
        cross(w).wait_recv()
        unit = y * 2 + x
        resid[w, unit] = (weight[w] * (keep[w] + xrecv[w].astype(F32))).astype(BF16)
        start(ag(w, 0, unit, across))
        start(ag(w, 1, unit, up))
        start(ag(w, 2, unit, down))

    def share(w):
        unit = y * 2 + 1 - x
        ag(w, 0, unit, across).wait_recv()
        start(ag(w, 3, unit, up))
        start(ag(w, 4, unit, down))

    def forward(w):
        ag(w, 1, ym * 2, up).wait_recv()
        start(ag(w, 5, ym * 2, up))
        ag(w, 1, yp * 2 + 1, down).wait_recv()
        start(ag(w, 6, yp * 2 + 1, down))

    def consume(w):
        for unit in (ym * 2 + 1, yp * 2, y2 * 2, y2 * 2 + 1):
            ag(w, 1, unit, up).wait_recv()
        block = resid[w].reshape(ROWS, NS)
        i_ = lax.broadcasted_iota(jnp.int32, (ROWS, ROWS), 0)
        j_ = lax.broadcasted_iota(jnp.int32, (ROWS, ROWS), 1)
        lo, hi = w * ROWS, (w + 1) * ROWS
        middle = block[:, lo:hi]
        zero = jnp.zeros_like(middle)
        upper = jnp.where(i_ <= j_, middle, zero)
        lower = jnp.where(i_ > j_, middle, zero)
        if w + 1 < WAVES:
            upper = jnp.concatenate([upper, block[:, hi:]], axis=1)
        if w > 0:
            lower = jnp.concatenate([block[:, :lo], lower], axis=1)
        rows = pl.ds(lo, ROWS)
        width = g.shape[3]
        step = min(256, width)
        for h in range(2):
            for t in range(width // step):
                cols = pl.ds(t * step, step)
                gr_u, gi_u = g[h, 0, lo:, cols], g[h, 1, lo:, cols]
                gr_l, gi_l = g[h, 0, :hi, cols], g[h, 1, :hi, cols]
                zr = dot_nn(upper, gr_u) - dot_nn(lower, gi_l)
                zi = dot_nn(upper, gi_u) + dot_nn(lower, gr_l)
                value = g[h, 0, rows, cols].astype(F32) * zr + g[h, 1, rows, cols].astype(F32) * zi
                value = jnp.sum(value, axis=0, keepdims=True)
                if w > 0:
                    value = value + sens[h, :, cols]
                sens[h, :, cols] = value

    stages = (produce, pass_on, collect, finish, share, forward, consume)
    for slot in range(WAVES + len(stages) - 1):
        for s, stage in enumerate(stages):
            if 0 <= slot - s < WAVES:
                stage(slot - s)

    f_copies = []
    me = q * 2 + core
    for n, (d, h) in enumerate(peers):
        to_q = lax.rem(q + d, nfreq)
        fsend[n] = basis[core, to_q] * sens[h]
        f_copies.append(remote(fsend.at[n], frecv.at[me], f_send.at[n], f_recv.at[n], peer(d, h)))
        f_copies[-1].start()
    frecv[me] = basis[core, q] * sens[0]
    for copy in f_copies:
        copy.wait_recv()
    total = frecv[0]
    for n in range(1, 2 * nfreq):
        total = total + frecv[n]
    out[...] = total

    for copy in c_copies + swap + sent + f_copies:
        copy.wait_send()


def on_device(green, coeffs, basis, amplitude, block_mask):
    nfreq = lax.axis_size("freq")
    cells = green.shape[3]
    dma = pltpu.SemaphoreType.DMA
    n = 2 * nfreq - 1
    return pl.pallas_call(
        functools.partial(kernel, nfreq),
        out_shape=jax.ShapeDtypeStruct((1, cells), F32),
        in_specs=[
            pl.BlockSpec(memory_space=pl.ANY),
            pl.BlockSpec(memory_space=pltpu.VMEM),
            pl.BlockSpec(memory_space=pltpu.SMEM),
            pl.BlockSpec(memory_space=pltpu.VMEM),
            pl.BlockSpec(memory_space=pltpu.SMEM),
        ],
        out_specs=pl.BlockSpec(memory_space=pltpu.VMEM),
        scratch_shapes=[
            pltpu.VMEM((2, 2, NS, cells), BF16),
            pltpu.VMEM((nfreq, 2, 1, cells), F32),
            pltpu.VMEM((2, 2, ROWS, cells), BF16),
            pltpu.VMEM((WAVES, 8, UNIT, NS), BF16),
            pltpu.VMEM((WAVES, 2, UNIT, NS), BF16),
            pltpu.VMEM((WAVES, 2, UNIT, NS), BF16),
            pltpu.VMEM((WAVES, 2, UNIT, NS), BF16),
            pltpu.VMEM((WAVES, 2, UNIT, NS), BF16),
            pltpu.VMEM((WAVES, UNIT, NS), BF16),
            pltpu.VMEM((WAVES, UNIT, NS), BF16),
            pltpu.VMEM((WAVES, UNIT, NS), F32),
            pltpu.VMEM((WAVES, 8, UNIT, NS), BF16),
            pltpu.VMEM((WAVES, UNIT, NS), F32),
            pltpu.VMEM((2, 1, cells), F32),
            pltpu.VMEM((n, 1, cells), F32),
            pltpu.VMEM((2 * nfreq, 1, cells), F32),
            dma((2,)),
            dma((2,)),
            dma((2,)),
            dma((n,)),
            dma((n,)),
            dma((WAVES, 4, 2)),
            dma((WAVES, 4, 2)),
            dma((WAVES, 7)),
            dma((WAVES, 8)),
            dma((n,)),
            dma((n,)),
        ],
        compiler_params=pltpu.CompilerParams(
            collective_id=0, has_side_effects=True, vmem_limit_bytes=48 * 1024 * 1024
        ),
        name="hessian_vector",
    )(green, coeffs, basis, amplitude, block_mask)


def solution(mesh):
    placed = (
        P(None, "freq", None, "cell"),
        P("freq", "cell"),
        P("freq", None),
        P("freq", None),
        P(),
    )
    return jax.shard_map(
        on_device, mesh=mesh, in_specs=placed, out_specs=P("freq", "cell"), check_vma=False
    )
```

```python
import functools

import jax
import jax.numpy as jnp
from jax import lax
from jax.experimental import pallas as pl
from jax.experimental.pallas import tpu as pltpu
from jax.sharding import PartitionSpec as P

MESH = pl.DeviceIdType.MESH
F32, BF16 = jnp.float32, jnp.bfloat16
NS = 1024
ROWS = 128
UNIT = ROWS // 8
HALF = NS // 2
KINDS = "ABABABAB"
GROUPS = ((0, 2), (2, 4), (4, 6), (6, 8))
CHUNKS = len(KINDS)
BLOCKS = 16
WIDTH = NS // BLOCKS


def dot_nt(a, b):
    return lax.dot_general(a, b, (((1,), (1,)), ((), ())), preferred_element_type=F32)


def dot_nn(a, b):
    return lax.dot_general(a, b, (((1,), (0,)), ((), ())), preferred_element_type=F32)


def kernel(
    nfreq,
    green,
    coeffs,
    basis_in,
    amp_in,
    mask_in,
    out,
    basis,
    amp,
    mask,
    g,
    cbuf,
    sc,
    part,
    resid,
    weight,
    keep,
    m1,
    m2,
    m3,
    relay,
    xsend,
    xrecv,
    bx,
    bsum,
    b1,
    b2,
    b3,
    bhold,
    brelay,
    sens,
    fsend,
    frecv,
    in_sem,
    own_sem,
    swap_send,
    swap_recv,
    c_send,
    c_recv,
    rs_send,
    rs_recv,
    ag_send,
    ag_recv,
    bx_send,
    bx_recv,
    by_send,
    by_recv,
    bg_send,
    bg_recv,
    f_send,
    f_recv,
):
    q = lax.axis_index("freq")
    cell = lax.axis_index("cell")
    core = lax.rem(cell, 2)
    y = lax.rem(lax.div(cell, 2), 4)
    x = lax.div(cell, 8)
    yp, ym, y2 = lax.rem(y + 1, 4), lax.rem(y + 3, 4), lax.rem(y + 2, 4)

    def at(x_, y_, core_):
        return {"freq": q, "cell": x_ * 8 + y_ * 2 + core_}

    up, down = at(x, yp, core), at(x, ym, core)
    across, twin = at(1 - x, y, core), at(x, y, 1 - core)

    peers = [(d, h) for d in range(nfreq) for h in range(2) if (d, h) != (0, 0)]

    def peer(d, h):
        to_core = core if h == 0 else 1 - core
        to_q = lax.rem(q + d, nfreq)
        return {"freq": to_q, "cell": x * 8 + y * 2 + to_core}

    def remote(src, dst, send, recv, device):
        return pltpu.make_async_remote_copy(
            src_ref=src,
            dst_ref=dst,
            send_sem=send,
            recv_sem=recv,
            device_id=device,
            device_id_type=MESH,
        )

    small = [
        pltpu.make_async_copy(basis_in, basis, in_sem.at[0]),
        pltpu.make_async_copy(amp_in, amp, in_sem.at[1]),
        pltpu.make_async_copy(mask_in, mask, in_sem.at[2]),
        pltpu.make_async_copy(coeffs, cbuf.at[q, 0], in_sem.at[3]),
    ]
    for copy in small:
        copy.start()
    own = [pltpu.make_async_copy(green.at[p, core], g.at[0, p], own_sem.at[p]) for p in range(2)]
    for copy in own:
        copy.start()

    barrier = pltpu.get_barrier_semaphore()
    met = [peer(d, h) for d, h in peers] + [up, down, across]
    for device in met:
        pl.semaphore_signal(barrier, inc=1, device_id=device, device_id_type=MESH)

    for copy in small:
        copy.wait()

    lane = lax.broadcasted_iota(jnp.int32, (1, NS), 1)
    block_of = lane // WIDTH
    amp_row = amp[pl.ds(core, 1), :]
    for w in range(CHUNKS):
        first = w * ROWS + (y * 2 + x) * UNIT
        a = lax.div(first, WIDTH)
        pair = jnp.zeros((1, NS), F32)
        for b in range(BLOCKS):
            m = (mask[a, b] + mask[b, a]).astype(F32)
            pair = pair + jnp.where(block_of == b, m, 0.0)
        row = lax.broadcasted_iota(jnp.int32, (UNIT, NS), 0) + first
        col = lax.broadcasted_iota(jnp.int32, (UNIT, NS), 1)
        same = row == col
        amp_col = jnp.sum(jnp.where(same, amp_row, 0.0), axis=1, keepdims=True)
        weight[w] = jnp.where(same, 0.5, 1.0) * (amp_col * (amp_row * pair))

    pl.semaphore_wait(barrier, len(met))

    c_copies = []
    for n, (d, h) in enumerate(peers):
        c_copies.append(
            remote(coeffs, cbuf.at[q, h], c_send.at[n], c_recv.at[n], peer(d, h))
        )
        c_copies[-1].start()
    swap = [
        remote(green.at[p, 1 - core], g.at[1, p], swap_send.at[p], swap_recv.at[p], twin)
        for p in range(2)
    ]
    for copy in swap:
        copy.start()

    for copy in c_copies:
        copy.wait_recv()
    source = []
    for h in range(2):
        total = basis[core, 0] * cbuf[0, h]
        for b in range(1, nfreq):
            total = total + basis[core, b] * cbuf[b, h]
        source.append(total)

    for copy in own:
        copy.wait()
    for copy in swap:
        copy.wait_recv()

    sent = []

    def start(copy):
        copy.start()
        sent.append(copy)

    def rs_up(w, n, src, dst):
        return remote(src, dst, rs_send.at[w, n, 0], rs_recv.at[w, n, 0], up)

    def rs_down(w, n, src, dst):
        return remote(src, dst, rs_send.at[w, n, 1], rs_recv.at[w, n, 1], down)

    def ag(w, n, unit, device):
        ref = resid.at[w, unit]
        return remote(ref, ref, ag_send.at[w, n], ag_recv.at[w, unit], device)

    def produce(group):
        c0, c1 = group
        lo, hi = c0 * ROWS, c1 * ROWS
        count = hi - lo
        for h in range(2):
            for p in range(2):
                field = g[h, p, lo:hi, :].astype(F32)
                sc[h, p, :count, :] = (field * source[h]).astype(BF16)

        def real(start, stop):
            total = dot_nt(sc[0, 0, :count], g[0, 0, start:stop])
            total += dot_nt(sc[0, 1, :count], g[0, 1, start:stop])
            total += dot_nt(sc[1, 0, :count], g[1, 0, start:stop])
            total += dot_nt(sc[1, 1, :count], g[1, 1, start:stop])
            return total

        def imag(start, stop):
            plus = dot_nt(sc[0, 1, :count], g[0, 0, start:stop])
            plus += dot_nt(sc[1, 1, :count], g[1, 0, start:stop])
            minus = dot_nt(sc[0, 0, :count], g[0, 1, start:stop])
            minus += dot_nt(sc[1, 0, :count], g[1, 1, start:stop])
            return plus - minus

        def put(start, stop, block):
            shape = (c1 - c0, 8, UNIT, stop - start)
            part[c0:c1, :, :, start:stop] = block.astype(BF16).reshape(shape)

        for start in range(0, lo, 256):
            stop = min(start + 256, lo)
            put(start, stop, imag(start, stop))
        i_ = lax.broadcasted_iota(jnp.int32, (count, count), 0)
        j_ = lax.broadcasted_iota(jnp.int32, (count, count), 1)
        put(lo, hi, jnp.where(i_ <= j_, real(lo, hi), imag(lo, hi)))
        for start in range(hi, NS, 256):
            stop = min(start + 256, NS)
            put(start, stop, real(start, stop))
        for c in range(c0, c1):
            if KINDS[c] == "A":
                start_a(c)
            else:
                start_b(c)

    def start_a(w):
        start(rs_up(w, 0, part.at[w, y2 * 2], m1.at[w, 0]))
        start(rs_down(w, 0, part.at[w, y2 * 2 + 1], m1.at[w, 1]))
        start(rs_up(w, 1, part.at[w, yp * 2 + 1], m2.at[w, 0]))
        start(rs_down(w, 1, part.at[w, ym * 2], m2.at[w, 1]))

    targets = (y2, yp, ym, y)

    def b_cross(w, r):
        src = part.at[w, targets[r] * 2 + 1 - x]
        return remote(src, bx.at[w, r], bx_send.at[w, r], bx_recv.at[w, r], across)

    def b_up(w, n, src, dst):
        return remote(src, dst, by_send.at[w, n, 0], by_recv.at[w, n, 0], up)

    def b_down(w, n, src, dst):
        return remote(src, dst, by_send.at[w, n, 1], by_recv.at[w, n, 1], down)

    def left(ref):
        return ref.at[:, 0:HALF]

    def right(ref):
        return ref.at[:, HALF:NS]

    def b_share(w, role, ref, device):
        return remote(ref, ref, bg_send.at[w, role], bg_recv.at[w, role], device)

    def b_unit(w, t):
        return resid.at[w, t * 2 + x]

    def start_b(w):
        for r in range(4):
            start(b_cross(w, r))

    def b_sum(w):
        def total(r):
            b_cross(w, r).wait_recv()
            return part[w, targets[r] * 2 + x].astype(F32) + bx[w, r].astype(F32)

        bsum[w, 0] = total(0).astype(BF16)
        start(b_up(w, 0, left(bsum.at[w, 0]), b1.at[w, 0]))
        start(b_down(w, 0, right(bsum.at[w, 0]), b1.at[w, 1]))
        value = total(1)
        bhold[w, 0] = value[:, :HALF]
        bsum[w, 1, :, HALF:] = value[:, HALF:].astype(BF16)
        start(b_up(w, 1, right(bsum.at[w, 1]), b2.at[w, 0]))
        value = total(2)
        bhold[w, 1] = value[:, HALF:]
        bsum[w, 2, :, :HALF] = value[:, :HALF].astype(BF16)
        start(b_down(w, 1, left(bsum.at[w, 2]), b2.at[w, 1]))
        keep[w] = total(3)

    def b_pass_on(w):
        b_up(w, 0, left(bsum.at[w, 0]), b1.at[w, 0]).wait_recv()
        brelay[w, 0] = (bhold[w, 0] + b1[w, 0].astype(F32)).astype(BF16)
        start(b_up(w, 2, brelay.at[w, 0], b3.at[w, 0]))
        b_down(w, 0, right(bsum.at[w, 0]), b1.at[w, 1]).wait_recv()
        brelay[w, 1] = (bhold[w, 1] + b1[w, 1].astype(F32)).astype(BF16)
        start(b_down(w, 2, brelay.at[w, 1], b3.at[w, 1]))

    def b_finish(w):
        b_up(w, 1, right(bsum.at[w, 1]), b2.at[w, 0]).wait_recv()
        b_down(w, 1, left(bsum.at[w, 2]), b2.at[w, 1]).wait_recv()
        b_up(w, 2, brelay.at[w, 0], b3.at[w, 0]).wait_recv()
        b_down(w, 2, brelay.at[w, 1], b3.at[w, 1]).wait_recv()
        low = keep[w, :, :HALF] + b3[w, 0].astype(F32) + b2[w, 1].astype(F32)
        high = keep[w, :, HALF:] + b3[w, 1].astype(F32) + b2[w, 0].astype(F32)
        unit = y * 2 + x
        resid[w, unit, :, :HALF] = (weight[w, :, :HALF] * low).astype(BF16)
        resid[w, unit, :, HALF:] = (weight[w, :, HALF:] * high).astype(BF16)
        start(b_share(w, 0, b_unit(w, y), up))
        start(b_share(w, 1, b_unit(w, y), down))
        start(b_share(w, 4, b_unit(w, y), across))

    def b_forward(w):
        b_share(w, 0, b_unit(w, ym), up).wait_recv()
        start(b_share(w, 2, left(b_unit(w, ym)), up))
        start(b_share(w, 5, b_unit(w, ym), across))
        b_share(w, 1, b_unit(w, yp), down).wait_recv()
        start(b_share(w, 3, right(b_unit(w, yp)), down))
        start(b_share(w, 6, b_unit(w, yp), across))

    def b_last(w):
        b_share(w, 2, left(b_unit(w, y2)), up).wait_recv()
        b_share(w, 3, right(b_unit(w, y2)), down).wait_recv()
        start(b_share(w, 7, b_unit(w, y2), across))

    def pass_on(w):
        rs_up(w, 0, part.at[w, y2 * 2], m1.at[w, 0]).wait_recv()
        relay[w, 0] = (part[w, yp * 2].astype(F32) + m1[w, 0].astype(F32)).astype(BF16)
        start(rs_up(w, 2, relay.at[w, 0], m3.at[w, 0]))
        rs_down(w, 0, part.at[w, y2 * 2 + 1], m1.at[w, 1]).wait_recv()
        relay[w, 1] = (part[w, ym * 2 + 1].astype(F32) + m1[w, 1].astype(F32)).astype(BF16)
        start(rs_down(w, 2, relay.at[w, 1], m3.at[w, 1]))

    def cross(w):
        return remote(xsend.at[w], xrecv.at[w], rs_send.at[w, 3, 0], rs_recv.at[w, 3, 0], across)

    def collect(w):
        rs_up(w, 1, part.at[w, yp * 2 + 1], m2.at[w, 0]).wait_recv()
        rs_down(w, 1, part.at[w, ym * 2], m2.at[w, 1]).wait_recv()
        rs_up(w, 2, relay.at[w, 0], m3.at[w, 0]).wait_recv()
        rs_down(w, 2, relay.at[w, 1], m3.at[w, 1]).wait_recv()
        low = part[w, y * 2].astype(F32) + m3[w, 0].astype(F32) + m2[w, 1].astype(F32)
        high = part[w, y * 2 + 1].astype(F32) + m3[w, 1].astype(F32) + m2[w, 0].astype(F32)
        mine = x == 0
        xsend[w] = jnp.where(mine, high, low).astype(BF16)
        start(cross(w))
        keep[w] = jnp.where(mine, low, high)

    def finish(w):
        cross(w).wait_recv()
        unit = y * 2 + x
        resid[w, unit] = (weight[w] * (keep[w] + xrecv[w].astype(F32))).astype(BF16)
        start(ag(w, 0, unit, across))
        start(ag(w, 1, unit, up))
        start(ag(w, 2, unit, down))

    def share(w):
        unit = y * 2 + 1 - x
        ag(w, 0, unit, across).wait_recv()
        start(ag(w, 3, unit, up))
        start(ag(w, 4, unit, down))

    def forward(w):
        ag(w, 1, ym * 2, up).wait_recv()
        start(ag(w, 5, ym * 2, up))
        ag(w, 1, yp * 2 + 1, down).wait_recv()
        start(ag(w, 6, yp * 2 + 1, down))

    def arrived(w):
        if KINDS[w] == "A":
            for unit in (ym * 2 + 1, yp * 2, y2 * 2, y2 * 2 + 1):
                ag(w, 1, unit, up).wait_recv()
        else:
            for role in range(4, 8):
                b_share(w, role, b_unit(w, y), across).wait_recv()

    def consume(group):
        c0, c1 = group
        lo, hi = c0 * ROWS, c1 * ROWS
        count = hi - lo
        for c in range(c0, c1):
            arrived(c)
        block = resid[c0:c1].reshape(count, NS)
        i_ = lax.broadcasted_iota(jnp.int32, (count, count), 0)
        j_ = lax.broadcasted_iota(jnp.int32, (count, count), 1)
        middle = block[:, lo:hi]
        zero = jnp.zeros_like(middle)
        upper = jnp.where(i_ <= j_, middle, zero)
        lower = jnp.where(i_ > j_, middle, zero)
        if hi < NS:
            upper = jnp.concatenate([upper, block[:, hi:]], axis=1)
        if lo > 0:
            lower = jnp.concatenate([block[:, :lo], lower], axis=1)
        width = g.shape[3]
        step = min(256, width)
        for h in range(2):
            for t in range(width // step):
                cols = slice(t * step, (t + 1) * step)
                zr = dot_nn(upper, g[h, 0, lo:, cols]) - dot_nn(lower, g[h, 1, :hi, cols])
                zi = dot_nn(upper, g[h, 1, lo:, cols]) + dot_nn(lower, g[h, 0, :hi, cols])
                value = g[h, 0, lo:hi, cols].astype(F32) * zr
                value += g[h, 1, lo:hi, cols].astype(F32) * zi
                value = jnp.sum(value, axis=0, keepdims=True)
                if lo > 0:
                    value = value + sens[h, :, cols]
                sens[h, :, cols] = value

    def step_of(fa, fb):
        def run(group):
            for c in range(*group):
                (fa if KINDS[c] == "A" else fb)(c)

        return run

    stages = (
        produce,
        step_of(pass_on, b_sum),
        step_of(collect, b_pass_on),
        step_of(finish, b_finish),
        step_of(share, b_forward),
        step_of(forward, b_last),
        consume,
    )
    for slot in range(len(GROUPS) + len(stages) - 1):
        for n, stage in enumerate(stages):
            if 0 <= slot - n < len(GROUPS):
                stage(GROUPS[slot - n])

    f_copies = []
    me = q * 2 + core
    for n, (d, h) in enumerate(peers):
        to_q = lax.rem(q + d, nfreq)
        fsend[n] = basis[core, to_q] * sens[h]
        f_copies.append(remote(fsend.at[n], frecv.at[me], f_send.at[n], f_recv.at[n], peer(d, h)))
        f_copies[-1].start()
    frecv[me] = basis[core, q] * sens[0]
    for copy in f_copies:
        copy.wait_recv()
    total = frecv[0]
    for n in range(1, 2 * nfreq):
        total = total + frecv[n]
    out[...] = total

    for copy in c_copies + swap + sent + f_copies:
        copy.wait_send()


def on_device(green, coeffs, basis, amplitude, block_mask):
    nfreq = lax.axis_size("freq")
    cells = green.shape[3]
    dma = pltpu.SemaphoreType.DMA
    n = 2 * nfreq - 1
    return pl.pallas_call(
        functools.partial(kernel, nfreq),
        out_shape=jax.ShapeDtypeStruct((1, cells), F32),
        in_specs=[pl.BlockSpec(memory_space=pltpu.HBM)] * 5,
        out_specs=pl.BlockSpec(memory_space=pltpu.VMEM),
        scratch_shapes=[
            pltpu.SMEM(basis.shape, F32),
            pltpu.VMEM(amplitude.shape, F32),
            pltpu.SMEM(block_mask.shape, jnp.int32),
            pltpu.VMEM((2, 2, NS, cells), BF16),
            pltpu.VMEM((nfreq, 2, 1, cells), F32),
            pltpu.VMEM((2, 2, 2 * ROWS, cells), BF16),
            pltpu.VMEM((CHUNKS, 8, UNIT, NS), BF16),
            pltpu.VMEM((CHUNKS, 8, UNIT, NS), BF16),
            pltpu.VMEM((CHUNKS, UNIT, NS), F32),
            pltpu.VMEM((CHUNKS, UNIT, NS), F32),
            pltpu.VMEM((CHUNKS, 2, UNIT, NS), BF16),
            pltpu.VMEM((CHUNKS, 2, UNIT, NS), BF16),
            pltpu.VMEM((CHUNKS, 2, UNIT, NS), BF16),
            pltpu.VMEM((CHUNKS, 2, UNIT, NS), BF16),
            pltpu.VMEM((CHUNKS, UNIT, NS), BF16),
            pltpu.VMEM((CHUNKS, UNIT, NS), BF16),
            pltpu.VMEM((CHUNKS, 4, UNIT, NS), BF16),
            pltpu.VMEM((CHUNKS, 3, UNIT, NS), BF16),
            pltpu.VMEM((CHUNKS, 2, UNIT, HALF), BF16),
            pltpu.VMEM((CHUNKS, 2, UNIT, HALF), BF16),
            pltpu.VMEM((CHUNKS, 2, UNIT, HALF), BF16),
            pltpu.VMEM((CHUNKS, 2, UNIT, HALF), F32),
            pltpu.VMEM((CHUNKS, 2, UNIT, HALF), BF16),
            pltpu.VMEM((2, 1, cells), F32),
            pltpu.VMEM((n, 1, cells), F32),
            pltpu.VMEM((2 * nfreq, 1, cells), F32),
            dma((4,)),
            dma((2,)),
            dma((2,)),
            dma((2,)),
            dma((n,)),
            dma((n,)),
            dma((CHUNKS, 4, 2)),
            dma((CHUNKS, 4, 2)),
            dma((CHUNKS, 7)),
            dma((CHUNKS, 8)),
            dma((CHUNKS, 4)),
            dma((CHUNKS, 4)),
            dma((CHUNKS, 3, 2)),
            dma((CHUNKS, 3, 2)),
            dma((CHUNKS, 8)),
            dma((CHUNKS, 8)),
            dma((n,)),
            dma((n,)),
        ],
        compiler_params=pltpu.CompilerParams(
            collective_id=0, has_side_effects=True, vmem_limit_bytes=67043328
        ),
        name="hessian_vector",
    )(green, coeffs, basis, amplitude, block_mask)


def solution(mesh):
    placed = (
        P(None, "freq", None, "cell"),
        P("freq", "cell"),
        P("freq", None),
        P("freq", None),
        P(),
    )
    return jax.shard_map(
        on_device, mesh=mesh, in_specs=placed, out_specs=P("freq", "cell"), check_vma=False
    )
```

```python
import functools

import jax
import jax.numpy as jnp
from jax import lax
from jax.experimental import pallas as pl
from jax.experimental.pallas import tpu as pltpu
from jax.sharding import PartitionSpec as P

MESH = pl.DeviceIdType.MESH
F32, BF16 = jnp.float32, jnp.bfloat16
NS = 1024
ROWS = 128
UNIT = ROWS // 8
HALF = NS // 2
KINDS = "BAABABAB"
GROUPS = ((0, 2), (2, 4), (4, 6), (6, 8))
CHUNKS = len(KINDS)
ORDER = (
    ("P", 0), ("P", 1), ("P", 2), ("B0", 0), ("A1u", 1), ("A1d", 1), ("P", 3), ("B3", 0),
    ("B1", 0), ("B2", 0), ("A1u", 2), ("A1d", 2), ("B0", 3), ("B1", 3), ("A1u", 4), ("A1d", 4),
    ("B2", 3), ("B4u", 0), ("B4d", 0), ("B3", 3), ("A2", 1), ("B0", 5), ("A1u", 6), ("A1d", 6),
    ("B1", 5), ("B2", 5), ("B3", 5), ("A2", 2), ("B4u", 3), ("B4d", 3), ("B0", 7), ("B1", 7),
    ("A2", 4), ("B5", 0), ("B2", 7), ("B4u", 5), ("B4d", 5), ("B3", 7), ("A2", 6), ("A3", 1),
    ("B5", 3), ("B4u", 7), ("B4d", 7), ("A3", 2), ("A3", 4), ("B6u", 0), ("B6d", 0), ("B5", 5),
    ("A3", 6), ("A4", 1), ("B6u", 3), ("B6d", 3), ("B5", 7), ("A4", 2), ("A4", 4), ("B7", 0),
    ("B6u", 5), ("B6d", 5), ("A5u", 1), ("A5d", 1), ("A4", 6), ("B7", 3), ("B6u", 7),
    ("B6d", 7), ("A5u", 2), ("A5d", 2), ("A5u", 4), ("A5d", 4), ("B7", 5), ("C", 0), ("A5u", 6),
    ("A5d", 6), ("B7", 7), ("C", 1), ("C", 2), ("C", 3),
)
BLOCKS = 16
WIDTH = NS // BLOCKS


def dot_nt(a, b):
    return lax.dot_general(a, b, (((1,), (1,)), ((), ())), preferred_element_type=F32)


def dot_nn(a, b):
    return lax.dot_general(a, b, (((1,), (0,)), ((), ())), preferred_element_type=F32)


def kernel(
    nfreq,
    green,
    coeffs,
    basis_in,
    amp_in,
    mask_in,
    out,
    basis,
    amp,
    mask,
    g,
    cbuf,
    sc,
    part,
    resid,
    weight,
    keep,
    m1,
    m2,
    m3,
    relay,
    xsend,
    xrecv,
    bx,
    bsum,
    b1,
    b2,
    b3,
    bhold,
    brelay,
    sens,
    fsend,
    frecv,
    in_sem,
    own_sem,
    swap_send,
    swap_recv,
    c_send,
    c_recv,
    rs_send,
    rs_recv,
    ag_send,
    ag_recv,
    bx_send,
    bx_recv,
    by_send,
    by_recv,
    bg_send,
    bg_recv,
    f_send,
    f_recv,
):
    q = lax.axis_index("freq")
    cell = lax.axis_index("cell")
    core = lax.rem(cell, 2)
    y = lax.rem(lax.div(cell, 2), 4)
    x = lax.div(cell, 8)
    yp, ym, y2 = lax.rem(y + 1, 4), lax.rem(y + 3, 4), lax.rem(y + 2, 4)

    def at(x_, y_, core_):
        return {"freq": q, "cell": x_ * 8 + y_ * 2 + core_}

    up, down = at(x, yp, core), at(x, ym, core)
    across, twin = at(1 - x, y, core), at(x, y, 1 - core)

    far_first = sorted(range(nfreq), key=lambda d: (d % 4 != 2, d % 2 == 0, d == 0))
    peers = [(d, h) for d in far_first for h in (1, 0) if (d, h) != (0, 0)]

    def peer(d, h):
        to_core = core if h == 0 else 1 - core
        to_q = lax.rem(q + d, nfreq)
        return {"freq": to_q, "cell": x * 8 + y * 2 + to_core}

    def remote(src, dst, send, recv, device):
        return pltpu.make_async_remote_copy(
            src_ref=src,
            dst_ref=dst,
            send_sem=send,
            recv_sem=recv,
            device_id=device,
            device_id_type=MESH,
        )

    small = [
        pltpu.make_async_copy(basis_in, basis, in_sem.at[0]),
        pltpu.make_async_copy(amp_in, amp, in_sem.at[1]),
        pltpu.make_async_copy(mask_in, mask, in_sem.at[2]),
        pltpu.make_async_copy(coeffs, cbuf.at[q, 0], in_sem.at[3]),
    ]
    for copy in small:
        copy.start()
    own = [pltpu.make_async_copy(green.at[p, core], g.at[0, p], own_sem.at[p]) for p in range(2)]
    for copy in own:
        copy.start()

    barrier = pltpu.get_barrier_semaphore()
    met = [peer(d, h) for d, h in peers] + [up, down, across]
    for device in met:
        pl.semaphore_signal(barrier, inc=1, device_id=device, device_id_type=MESH)

    for copy in small:
        copy.wait()

    lane = lax.broadcasted_iota(jnp.int32, (1, NS), 1)
    block_of = lane // WIDTH
    amp_row = amp[pl.ds(core, 1), :]
    for w in range(CHUNKS):
        first = w * ROWS + (y * 2 + x) * UNIT
        a = lax.div(first, WIDTH)
        pair = jnp.zeros((1, NS), F32)
        for b in range(BLOCKS):
            m = (mask[a, b] + mask[b, a]).astype(F32)
            pair = pair + jnp.where(block_of == b, m, 0.0)
        row = lax.broadcasted_iota(jnp.int32, (UNIT, NS), 0) + first
        col = lax.broadcasted_iota(jnp.int32, (UNIT, NS), 1)
        same = row == col
        amp_col = jnp.sum(jnp.where(same, amp_row, 0.0), axis=1, keepdims=True)
        weight[w] = jnp.where(same, 0.5, 1.0) * (amp_col * (amp_row * pair))

    pl.semaphore_wait(barrier, len(met))

    c_copies = []
    for n, (d, h) in enumerate(peers):
        c_copies.append(
            remote(coeffs, cbuf.at[q, h], c_send.at[n], c_recv.at[n], peer(d, h))
        )
        c_copies[-1].start()
    swap = [
        remote(green.at[p, 1 - core], g.at[1, p], swap_send.at[p], swap_recv.at[p], twin)
        for p in range(2)
    ]
    for copy in swap:
        copy.start()

    for copy in c_copies:
        copy.wait_recv()
    source = []
    for h in range(2):
        total = basis[core, 0] * cbuf[0, h]
        for b in range(1, nfreq):
            total = total + basis[core, b] * cbuf[b, h]
        source.append(total)

    for copy in own:
        copy.wait()
    for copy in swap:
        copy.wait_recv()

    sent = []

    def start(copy):
        copy.start()
        sent.append(copy)

    def rs_up(w, n, src, dst):
        return remote(src, dst, rs_send.at[w, n, 0], rs_recv.at[w, n, 0], up)

    def rs_down(w, n, src, dst):
        return remote(src, dst, rs_send.at[w, n, 1], rs_recv.at[w, n, 1], down)

    def ag(w, n, unit, device):
        ref = resid.at[w, unit]
        return remote(ref, ref, ag_send.at[w, n], ag_recv.at[w, unit], device)

    def produce(group):
        c0, c1 = group
        lo, hi = c0 * ROWS, c1 * ROWS
        count = hi - lo
        for h in range(2):
            for p in range(2):
                field = g[h, p, lo:hi, :].astype(F32)
                sc[h, p, :count, :] = (field * source[h]).astype(BF16)

        def real(start, stop):
            total = dot_nt(sc[0, 0, :count], g[0, 0, start:stop])
            total += dot_nt(sc[0, 1, :count], g[0, 1, start:stop])
            total += dot_nt(sc[1, 0, :count], g[1, 0, start:stop])
            total += dot_nt(sc[1, 1, :count], g[1, 1, start:stop])
            return total

        def imag(start, stop):
            plus = dot_nt(sc[0, 1, :count], g[0, 0, start:stop])
            plus += dot_nt(sc[1, 1, :count], g[1, 0, start:stop])
            minus = dot_nt(sc[0, 0, :count], g[0, 1, start:stop])
            minus += dot_nt(sc[1, 0, :count], g[1, 1, start:stop])
            return plus - minus

        def put(start, stop, block):
            shape = (c1 - c0, 8, UNIT, stop - start)
            part[c0:c1, :, :, start:stop] = block.astype(BF16).reshape(shape)

        for start in range(0, lo, 256):
            stop = min(start + 256, lo)
            put(start, stop, imag(start, stop))
        i_ = lax.broadcasted_iota(jnp.int32, (count, count), 0)
        j_ = lax.broadcasted_iota(jnp.int32, (count, count), 1)
        put(lo, hi, jnp.where(i_ <= j_, real(lo, hi), imag(lo, hi)))
        for start in range(hi, NS, 256):
            stop = min(start + 256, NS)
            put(start, stop, real(start, stop))
        for c in range(c0, c1):
            if KINDS[c] == "A":
                start_a(c)
            else:
                start_b(c)

    def start_a(w):
        start(rs_up(w, 0, part.at[w, y2 * 2], m1.at[w, 0]))
        start(rs_down(w, 0, part.at[w, y2 * 2 + 1], m1.at[w, 1]))
        start(rs_up(w, 1, part.at[w, yp * 2 + 1], m2.at[w, 0]))
        start(rs_down(w, 1, part.at[w, ym * 2], m2.at[w, 1]))

    targets = (y2, yp, ym, y)

    def b_cross(w, r):
        src = part.at[w, targets[r] * 2 + 1 - x]
        return remote(src, bx.at[w, r], bx_send.at[w, r], bx_recv.at[w, r], across)

    def b_up(w, n, src, dst):
        return remote(src, dst, by_send.at[w, n, 0], by_recv.at[w, n, 0], up)

    def b_down(w, n, src, dst):
        return remote(src, dst, by_send.at[w, n, 1], by_recv.at[w, n, 1], down)

    def left(ref):
        return ref.at[:, 0:HALF]

    def right(ref):
        return ref.at[:, HALF:NS]

    def b_share(w, role, ref, device):
        return remote(ref, ref, bg_send.at[w, role], bg_recv.at[w, role], device)

    def b_unit(w, t):
        return resid.at[w, t * 2 + x]

    def start_b(w):
        for r in range(4):
            start(b_cross(w, r))

    def b_total(w, r):
        b_cross(w, r).wait_recv()
        return part[w, targets[r] * 2 + x].astype(F32) + bx[w, r].astype(F32)

    def b_sum_far(w):
        bsum[w, 0] = b_total(w, 0).astype(BF16)
        start(b_up(w, 0, left(bsum.at[w, 0]), b1.at[w, 0]))
        start(b_down(w, 0, right(bsum.at[w, 0]), b1.at[w, 1]))

    def b_sum_up(w):
        value = b_total(w, 1)
        bhold[w, 0] = value[:, :HALF]
        bsum[w, 1, :, HALF:] = value[:, HALF:].astype(BF16)
        start(b_up(w, 1, right(bsum.at[w, 1]), b2.at[w, 0]))

    def b_sum_down(w):
        value = b_total(w, 2)
        bhold[w, 1] = value[:, HALF:]
        bsum[w, 2, :, :HALF] = value[:, :HALF].astype(BF16)
        start(b_down(w, 1, left(bsum.at[w, 2]), b2.at[w, 1]))

    def b_sum_own(w):
        keep[w] = b_total(w, 3)

    def b_relay_up(w):
        b_up(w, 0, left(bsum.at[w, 0]), b1.at[w, 0]).wait_recv()
        brelay[w, 0] = (bhold[w, 0] + b1[w, 0].astype(F32)).astype(BF16)
        start(b_up(w, 2, brelay.at[w, 0], b3.at[w, 0]))

    def b_relay_down(w):
        b_down(w, 0, right(bsum.at[w, 0]), b1.at[w, 1]).wait_recv()
        brelay[w, 1] = (bhold[w, 1] + b1[w, 1].astype(F32)).astype(BF16)
        start(b_down(w, 2, brelay.at[w, 1], b3.at[w, 1]))

    def b_finish(w):
        b_up(w, 1, right(bsum.at[w, 1]), b2.at[w, 0]).wait_recv()
        b_down(w, 1, left(bsum.at[w, 2]), b2.at[w, 1]).wait_recv()
        b_up(w, 2, brelay.at[w, 0], b3.at[w, 0]).wait_recv()
        b_down(w, 2, brelay.at[w, 1], b3.at[w, 1]).wait_recv()
        low = keep[w, :, :HALF] + b3[w, 0].astype(F32) + b2[w, 1].astype(F32)
        high = keep[w, :, HALF:] + b3[w, 1].astype(F32) + b2[w, 0].astype(F32)
        unit = y * 2 + x
        resid[w, unit, :, :HALF] = (weight[w, :, :HALF] * low).astype(BF16)
        resid[w, unit, :, HALF:] = (weight[w, :, HALF:] * high).astype(BF16)
        start(b_share(w, 0, b_unit(w, y), up))
        start(b_share(w, 1, b_unit(w, y), down))
        start(b_share(w, 4, b_unit(w, y), across))

    def b_forward_up(w):
        b_share(w, 0, b_unit(w, ym), up).wait_recv()
        start(b_share(w, 2, left(b_unit(w, ym)), up))
        start(b_share(w, 5, b_unit(w, ym), across))

    def b_forward_down(w):
        b_share(w, 1, b_unit(w, yp), down).wait_recv()
        start(b_share(w, 3, right(b_unit(w, yp)), down))
        start(b_share(w, 6, b_unit(w, yp), across))

    def b_last(w):
        b_share(w, 2, left(b_unit(w, y2)), up).wait_recv()
        b_share(w, 3, right(b_unit(w, y2)), down).wait_recv()
        start(b_share(w, 7, b_unit(w, y2), across))

    def a_relay_up(w):
        rs_up(w, 0, part.at[w, y2 * 2], m1.at[w, 0]).wait_recv()
        relay[w, 0] = (part[w, yp * 2].astype(F32) + m1[w, 0].astype(F32)).astype(BF16)
        start(rs_up(w, 2, relay.at[w, 0], m3.at[w, 0]))

    def a_relay_down(w):
        rs_down(w, 0, part.at[w, y2 * 2 + 1], m1.at[w, 1]).wait_recv()
        relay[w, 1] = (part[w, ym * 2 + 1].astype(F32) + m1[w, 1].astype(F32)).astype(BF16)
        start(rs_down(w, 2, relay.at[w, 1], m3.at[w, 1]))

    def cross(w):
        return remote(xsend.at[w], xrecv.at[w], rs_send.at[w, 3, 0], rs_recv.at[w, 3, 0], across)

    def collect(w):
        rs_up(w, 1, part.at[w, yp * 2 + 1], m2.at[w, 0]).wait_recv()
        rs_down(w, 1, part.at[w, ym * 2], m2.at[w, 1]).wait_recv()
        rs_up(w, 2, relay.at[w, 0], m3.at[w, 0]).wait_recv()
        rs_down(w, 2, relay.at[w, 1], m3.at[w, 1]).wait_recv()
        low = part[w, y * 2].astype(F32) + m3[w, 0].astype(F32) + m2[w, 1].astype(F32)
        high = part[w, y * 2 + 1].astype(F32) + m3[w, 1].astype(F32) + m2[w, 0].astype(F32)
        mine = x == 0
        xsend[w] = jnp.where(mine, high, low).astype(BF16)
        start(cross(w))
        keep[w] = jnp.where(mine, low, high)

    def finish(w):
        cross(w).wait_recv()
        unit = y * 2 + x
        resid[w, unit] = (weight[w] * (keep[w] + xrecv[w].astype(F32))).astype(BF16)
        start(ag(w, 0, unit, across))
        start(ag(w, 1, unit, up))
        start(ag(w, 2, unit, down))

    def share(w):
        unit = y * 2 + 1 - x
        ag(w, 0, unit, across).wait_recv()
        start(ag(w, 3, unit, up))
        start(ag(w, 4, unit, down))

    def forward_up(w):
        ag(w, 1, ym * 2, up).wait_recv()
        start(ag(w, 5, ym * 2, up))

    def forward_down(w):
        ag(w, 1, yp * 2 + 1, down).wait_recv()
        start(ag(w, 6, yp * 2 + 1, down))

    def arrived(w):
        if KINDS[w] == "A":
            for unit in (ym * 2 + 1, yp * 2, y2 * 2, y2 * 2 + 1):
                ag(w, 1, unit, up).wait_recv()
        else:
            for role in range(4, 8):
                b_share(w, role, b_unit(w, y), across).wait_recv()

    def consume(group):
        c0, c1 = group
        lo, hi = c0 * ROWS, c1 * ROWS
        count = hi - lo
        for c in range(c0, c1):
            arrived(c)
        block = resid[c0:c1].reshape(count, NS)
        i_ = lax.broadcasted_iota(jnp.int32, (count, count), 0)
        j_ = lax.broadcasted_iota(jnp.int32, (count, count), 1)
        middle = block[:, lo:hi]
        zero = jnp.zeros_like(middle)
        upper = jnp.where(i_ <= j_, middle, zero)
        lower = jnp.where(i_ > j_, middle, zero)
        if hi < NS:
            upper = jnp.concatenate([upper, block[:, hi:]], axis=1)
        if lo > 0:
            lower = jnp.concatenate([block[:, :lo], lower], axis=1)
        width = g.shape[3]
        step = min(256, width)
        for h in range(2):
            for t in range(width // step):
                cols = slice(t * step, (t + 1) * step)
                zr = dot_nn(upper, g[h, 0, lo:, cols]) - dot_nn(lower, g[h, 1, :hi, cols])
                zi = dot_nn(upper, g[h, 1, lo:, cols]) + dot_nn(lower, g[h, 0, :hi, cols])
                value = g[h, 0, lo:hi, cols].astype(F32) * zr
                value += g[h, 1, lo:hi, cols].astype(F32) * zi
                value = jnp.sum(value, axis=0, keepdims=True)
                if lo > 0:
                    value = value + sens[h, :, cols]
                sens[h, :, cols] = value

    ops = {
        "P": lambda n: produce(GROUPS[n]),
        "C": lambda n: consume(GROUPS[n]),
        "A1u": a_relay_up,
        "A1d": a_relay_down,
        "A2": collect,
        "A3": finish,
        "A4": share,
        "A5u": forward_up,
        "A5d": forward_down,
        "B0": b_sum_far,
        "B1": b_sum_up,
        "B2": b_sum_down,
        "B3": b_sum_own,
        "B4u": b_relay_up,
        "B4d": b_relay_down,
        "B5": b_finish,
        "B6u": b_forward_up,
        "B6d": b_forward_down,
        "B7": b_last,
    }
    for name, n in ORDER:
        ops[name](n)

    f_copies = []
    me = q * 2 + core
    for n, (d, h) in enumerate(peers):
        to_q = lax.rem(q + d, nfreq)
        fsend[n] = basis[core, to_q] * sens[h]
        f_copies.append(remote(fsend.at[n], frecv.at[me], f_send.at[n], f_recv.at[n], peer(d, h)))
        f_copies[-1].start()
    frecv[me] = basis[core, q] * sens[0]
    for copy in f_copies:
        copy.wait_recv()
    total = frecv[0]
    for n in range(1, 2 * nfreq):
        total = total + frecv[n]
    out[...] = total

    for copy in c_copies + swap + sent + f_copies:
        copy.wait_send()


def on_device(green, coeffs, basis, amplitude, block_mask):
    nfreq = lax.axis_size("freq")
    cells = green.shape[3]
    dma = pltpu.SemaphoreType.DMA
    n = 2 * nfreq - 1
    return pl.pallas_call(
        functools.partial(kernel, nfreq),
        out_shape=jax.ShapeDtypeStruct((1, cells), F32),
        in_specs=[pl.BlockSpec(memory_space=pltpu.HBM)] * 5,
        out_specs=pl.BlockSpec(memory_space=pltpu.VMEM),
        scratch_shapes=[
            pltpu.SMEM(basis.shape, F32),
            pltpu.VMEM(amplitude.shape, F32),
            pltpu.SMEM(block_mask.shape, jnp.int32),
            pltpu.VMEM((2, 2, NS, cells), BF16),
            pltpu.VMEM((nfreq, 2, 1, cells), F32),
            pltpu.VMEM((2, 2, 2 * ROWS, cells), BF16),
            pltpu.VMEM((CHUNKS, 8, UNIT, NS), BF16),
            pltpu.VMEM((CHUNKS, 8, UNIT, NS), BF16),
            pltpu.VMEM((CHUNKS, UNIT, NS), F32),
            pltpu.VMEM((CHUNKS, UNIT, NS), F32),
            pltpu.VMEM((CHUNKS, 2, UNIT, NS), BF16),
            pltpu.VMEM((CHUNKS, 2, UNIT, NS), BF16),
            pltpu.VMEM((CHUNKS, 2, UNIT, NS), BF16),
            pltpu.VMEM((CHUNKS, 2, UNIT, NS), BF16),
            pltpu.VMEM((CHUNKS, UNIT, NS), BF16),
            pltpu.VMEM((CHUNKS, UNIT, NS), BF16),
            pltpu.VMEM((CHUNKS, 4, UNIT, NS), BF16),
            pltpu.VMEM((CHUNKS, 3, UNIT, NS), BF16),
            pltpu.VMEM((CHUNKS, 2, UNIT, HALF), BF16),
            pltpu.VMEM((CHUNKS, 2, UNIT, HALF), BF16),
            pltpu.VMEM((CHUNKS, 2, UNIT, HALF), BF16),
            pltpu.VMEM((CHUNKS, 2, UNIT, HALF), F32),
            pltpu.VMEM((CHUNKS, 2, UNIT, HALF), BF16),
            pltpu.VMEM((2, 1, cells), F32),
            pltpu.VMEM((n, 1, cells), F32),
            pltpu.VMEM((2 * nfreq, 1, cells), F32),
            dma((4,)),
            dma((2,)),
            dma((2,)),
            dma((2,)),
            dma((n,)),
            dma((n,)),
            dma((CHUNKS, 4, 2)),
            dma((CHUNKS, 4, 2)),
            dma((CHUNKS, 7)),
            dma((CHUNKS, 8)),
            dma((CHUNKS, 4)),
            dma((CHUNKS, 4)),
            dma((CHUNKS, 3, 2)),
            dma((CHUNKS, 3, 2)),
            dma((CHUNKS, 8)),
            dma((CHUNKS, 8)),
            dma((n,)),
            dma((n,)),
        ],
        compiler_params=pltpu.CompilerParams(
            collective_id=0, has_side_effects=True, vmem_limit_bytes=67043328
        ),
        name="hessian_vector",
    )(green, coeffs, basis, amplitude, block_mask)


def solution(mesh):
    placed = (
        P(None, "freq", None, "cell"),
        P("freq", "cell"),
        P("freq", None),
        P("freq", None),
        P(),
    )
    return jax.shard_map(
        on_device, mesh=mesh, in_specs=placed, out_specs=P("freq", "cell"), check_vma=False
    )
```

```python
import functools

import jax
import jax.numpy as jnp
from jax import lax
from jax.experimental import pallas as pl
from jax.experimental.pallas import tpu as pltpu
from jax.sharding import PartitionSpec as P

MESH = pl.DeviceIdType.MESH
F32, BF16 = jnp.float32, jnp.bfloat16
NS = 1024
ROWS = 128
UNIT = ROWS // 8
HALF = NS // 2
KINDS = "BAABABAB"
GROUPS = ((0, 2), (2, 4), (4, 6), (6, 8))
CHUNKS = len(KINDS)
ORDER = (
    ("P", 0), ("P", 1), ("P", 2), ("B0", 0), ("A1u", 1), ("A1d", 1), ("P", 3), ("B3", 0),
    ("B1", 0), ("B2", 0), ("A1u", 2), ("A1d", 2), ("B0", 3), ("B1", 3), ("A1u", 4), ("A1d", 4),
    ("B2", 3), ("B4u", 0), ("B4d", 0), ("B3", 3), ("A2", 1), ("B0", 5), ("A1u", 6), ("A1d", 6),
    ("B1", 5), ("B2", 5), ("B3", 5), ("A2", 2), ("B4u", 3), ("B4d", 3), ("B0", 7), ("B1", 7),
    ("A2", 4), ("B5", 0), ("B2", 7), ("B4u", 5), ("B4d", 5), ("B3", 7), ("A2", 6), ("A3", 1),
    ("B5", 3), ("B4u", 7), ("B4d", 7), ("A3", 2), ("A3", 4), ("B6u", 0), ("B6d", 0), ("B5", 5),
    ("A3", 6), ("A4", 1), ("B6u", 3), ("B6d", 3), ("B5", 7), ("A4", 2), ("A4", 4), ("B7", 0),
    ("B6u", 5), ("B6d", 5), ("A5u", 1), ("A5d", 1), ("A4", 6), ("B7", 3), ("B6u", 7),
    ("B6d", 7), ("A5u", 2), ("A5d", 2), ("A5u", 4), ("A5d", 4), ("B7", 5), ("C", 0), ("A5u", 6),
    ("A5d", 6), ("B7", 7), ("C", 1), ("C", 2), ("C", 3),
)
BLOCKS = 16
WIDTH = NS // BLOCKS


def dot_nt(a, b):
    return lax.dot_general(a, b, (((1,), (1,)), ((), ())), preferred_element_type=F32)


def dot_nn(a, b):
    return lax.dot_general(a, b, (((1,), (0,)), ((), ())), preferred_element_type=F32)


def kernel(
    nfreq,
    green,
    coeffs,
    basis_in,
    amp_in,
    mask_in,
    out,
    basis,
    amp,
    mask,
    g,
    cbuf,
    sc,
    part,
    resid,
    weight,
    keep,
    m1,
    m2,
    m3,
    relay,
    xsend,
    xrecv,
    bx,
    bsum,
    b1,
    b2,
    b3,
    bhold,
    brelay,
    sens,
    fsend,
    frecv,
    in_sem,
    own_sem,
    swap_send,
    swap_recv,
    c_send,
    c_recv,
    rs_send,
    rs_recv,
    ag_send,
    ag_recv,
    bx_send,
    bx_recv,
    by_send,
    by_recv,
    bg_send,
    bg_recv,
    f_send,
    f_recv,
):
    q = lax.axis_index("freq")
    cell = lax.axis_index("cell")
    core = lax.rem(cell, 2)
    y = lax.rem(lax.div(cell, 2), 4)
    x = lax.div(cell, 8)
    yp, ym, y2 = lax.rem(y + 1, 4), lax.rem(y + 3, 4), lax.rem(y + 2, 4)

    def at(x_, y_, core_):
        return {"freq": q, "cell": x_ * 8 + y_ * 2 + core_}

    up, down = at(x, yp, core), at(x, ym, core)
    across, twin = at(1 - x, y, core), at(x, y, 1 - core)

    far_first = sorted(range(nfreq), key=lambda d: (d % 4 != 2, d % 2 == 0, d == 0))
    peers = [(d, h) for d in far_first for h in (1, 0) if (d, h) != (0, 0)]

    def peer(d, h):
        to_core = core if h == 0 else 1 - core
        to_q = lax.rem(q + d, nfreq)
        return {"freq": to_q, "cell": x * 8 + y * 2 + to_core}

    def remote(src, dst, send, recv, device):
        return pltpu.make_async_remote_copy(
            src_ref=src,
            dst_ref=dst,
            send_sem=send,
            recv_sem=recv,
            device_id=device,
            device_id_type=MESH,
        )

    small = [
        pltpu.make_async_copy(basis_in, basis, in_sem.at[0]),
        pltpu.make_async_copy(amp_in, amp, in_sem.at[1]),
        pltpu.make_async_copy(mask_in, mask, in_sem.at[2]),
        pltpu.make_async_copy(coeffs, cbuf.at[q, 0], in_sem.at[3]),
    ]
    for copy in small:
        copy.start()
    own = [pltpu.make_async_copy(green.at[p, core], g.at[0, p], own_sem.at[p]) for p in range(2)]
    for copy in own:
        copy.start()

    barrier = pltpu.get_barrier_semaphore()
    met = [peer(d, h) for d, h in peers] + [up, down, across]
    for device in met:
        pl.semaphore_signal(barrier, inc=1, device_id=device, device_id_type=MESH)

    small[3].wait()
    pl.semaphore_wait(barrier, len(met))

    c_copies = []
    for n, (d, h) in enumerate(peers):
        c_copies.append(
            remote(cbuf.at[q, 0], cbuf.at[q, h], c_send.at[n], c_recv.at[n], peer(d, h))
        )
        c_copies[-1].start()
    swap = [
        remote(green.at[p, 1 - core], g.at[1, p], swap_send.at[p], swap_recv.at[p], twin)
        for p in range(2)
    ]
    for copy in swap:
        copy.start()

    for copy in small[:3]:
        copy.wait()

    lane = lax.broadcasted_iota(jnp.int32, (1, NS), 1)
    block_of = lane // WIDTH
    amp_row = amp[pl.ds(core, 1), :]
    for w in range(CHUNKS):
        first = w * ROWS + (y * 2 + x) * UNIT
        a = lax.div(first, WIDTH)
        pair = jnp.zeros((1, NS), F32)
        for b in range(BLOCKS):
            m = (mask[a, b] + mask[b, a]).astype(F32)
            pair = pair + jnp.where(block_of == b, m, 0.0)
        row = lax.broadcasted_iota(jnp.int32, (UNIT, NS), 0) + first
        col = lax.broadcasted_iota(jnp.int32, (UNIT, NS), 1)
        same = row == col
        amp_col = jnp.sum(jnp.where(same, amp_row, 0.0), axis=1, keepdims=True)
        weight[w] = jnp.where(same, 0.5, 1.0) * (amp_col * (amp_row * pair))

    for copy in c_copies:
        copy.wait_recv()
    source = []
    for h in range(2):
        total = basis[core, 0] * cbuf[0, h]
        for b in range(1, nfreq):
            total = total + basis[core, b] * cbuf[b, h]
        source.append(total)

    for copy in own:
        copy.wait()
    for copy in swap:
        copy.wait_recv()

    sent = []

    def start(copy):
        copy.start()
        sent.append(copy)

    def rs_up(w, n, src, dst):
        return remote(src, dst, rs_send.at[w, n, 0], rs_recv.at[w, n, 0], up)

    def rs_down(w, n, src, dst):
        return remote(src, dst, rs_send.at[w, n, 1], rs_recv.at[w, n, 1], down)

    def ag(w, n, unit, device):
        ref = resid.at[w, unit]
        return remote(ref, ref, ag_send.at[w, n], ag_recv.at[w, unit], device)

    def produce(group):
        c0, c1 = group
        lo, hi = c0 * ROWS, c1 * ROWS
        count = hi - lo
        for h in range(2):
            for p in range(2):
                field = g[h, p, lo:hi, :].astype(F32)
                sc[h, p, :count, :] = (field * source[h]).astype(BF16)

        def real(start, stop):
            total = dot_nt(sc[0, 0, :count], g[0, 0, start:stop])
            total += dot_nt(sc[0, 1, :count], g[0, 1, start:stop])
            total += dot_nt(sc[1, 0, :count], g[1, 0, start:stop])
            total += dot_nt(sc[1, 1, :count], g[1, 1, start:stop])
            return total

        def imag(start, stop):
            plus = dot_nt(sc[0, 1, :count], g[0, 0, start:stop])
            plus += dot_nt(sc[1, 1, :count], g[1, 0, start:stop])
            minus = dot_nt(sc[0, 0, :count], g[0, 1, start:stop])
            minus += dot_nt(sc[1, 0, :count], g[1, 1, start:stop])
            return plus - minus

        def put(start, stop, block):
            shape = (c1 - c0, 8, UNIT, stop - start)
            part[c0:c1, :, :, start:stop] = block.astype(BF16).reshape(shape)

        for start in range(0, lo, 256):
            stop = min(start + 256, lo)
            put(start, stop, imag(start, stop))
        i_ = lax.broadcasted_iota(jnp.int32, (count, count), 0)
        j_ = lax.broadcasted_iota(jnp.int32, (count, count), 1)
        put(lo, hi, jnp.where(i_ <= j_, real(lo, hi), imag(lo, hi)))
        for start in range(hi, NS, 256):
            stop = min(start + 256, NS)
            put(start, stop, real(start, stop))
        for c in range(c0, c1):
            if KINDS[c] == "A":
                start_a(c)
            else:
                start_b(c)

    def start_a(w):
        start(rs_up(w, 0, part.at[w, y2 * 2], m1.at[w, 0]))
        start(rs_down(w, 0, part.at[w, y2 * 2 + 1], m1.at[w, 1]))
        start(rs_up(w, 1, part.at[w, yp * 2 + 1], m2.at[w, 0]))
        start(rs_down(w, 1, part.at[w, ym * 2], m2.at[w, 1]))

    targets = (y2, yp, ym, y)

    def b_cross(w, r):
        src = part.at[w, targets[r] * 2 + 1 - x]
        return remote(src, bx.at[w, r], bx_send.at[w, r], bx_recv.at[w, r], across)

    def b_up(w, n, src, dst):
        return remote(src, dst, by_send.at[w, n, 0], by_recv.at[w, n, 0], up)

    def b_down(w, n, src, dst):
        return remote(src, dst, by_send.at[w, n, 1], by_recv.at[w, n, 1], down)

    def left(ref):
        return ref.at[:, 0:HALF]

    def right(ref):
        return ref.at[:, HALF:NS]

    def b_share(w, role, ref, device):
        return remote(ref, ref, bg_send.at[w, role], bg_recv.at[w, role], device)

    def b_unit(w, t):
        return resid.at[w, t * 2 + x]

    def start_b(w):
        for r in range(4):
            start(b_cross(w, r))

    def b_total(w, r):
        b_cross(w, r).wait_recv()
        return part[w, targets[r] * 2 + x].astype(F32) + bx[w, r].astype(F32)

    def b_sum_far(w):
        bsum[w, 0] = b_total(w, 0).astype(BF16)
        start(b_up(w, 0, left(bsum.at[w, 0]), b1.at[w, 0]))
        start(b_down(w, 0, right(bsum.at[w, 0]), b1.at[w, 1]))

    def b_sum_up(w):
        value = b_total(w, 1)
        bhold[w, 0] = value[:, :HALF]
        bsum[w, 1, :, HALF:] = value[:, HALF:].astype(BF16)
        start(b_up(w, 1, right(bsum.at[w, 1]), b2.at[w, 0]))

    def b_sum_down(w):
        value = b_total(w, 2)
        bhold[w, 1] = value[:, HALF:]
        bsum[w, 2, :, :HALF] = value[:, :HALF].astype(BF16)
        start(b_down(w, 1, left(bsum.at[w, 2]), b2.at[w, 1]))

    def b_sum_own(w):
        keep[w] = b_total(w, 3)

    def b_relay_up(w):
        b_up(w, 0, left(bsum.at[w, 0]), b1.at[w, 0]).wait_recv()
        brelay[w, 0] = (bhold[w, 0] + b1[w, 0].astype(F32)).astype(BF16)
        start(b_up(w, 2, brelay.at[w, 0], b3.at[w, 0]))

    def b_relay_down(w):
        b_down(w, 0, right(bsum.at[w, 0]), b1.at[w, 1]).wait_recv()
        brelay[w, 1] = (bhold[w, 1] + b1[w, 1].astype(F32)).astype(BF16)
        start(b_down(w, 2, brelay.at[w, 1], b3.at[w, 1]))

    def b_finish(w):
        b_up(w, 1, right(bsum.at[w, 1]), b2.at[w, 0]).wait_recv()
        b_down(w, 1, left(bsum.at[w, 2]), b2.at[w, 1]).wait_recv()
        b_up(w, 2, brelay.at[w, 0], b3.at[w, 0]).wait_recv()
        b_down(w, 2, brelay.at[w, 1], b3.at[w, 1]).wait_recv()
        low = keep[w, :, :HALF] + b3[w, 0].astype(F32) + b2[w, 1].astype(F32)
        high = keep[w, :, HALF:] + b3[w, 1].astype(F32) + b2[w, 0].astype(F32)
        unit = y * 2 + x
        resid[w, unit, :, :HALF] = (weight[w, :, :HALF] * low).astype(BF16)
        resid[w, unit, :, HALF:] = (weight[w, :, HALF:] * high).astype(BF16)
        start(b_share(w, 0, b_unit(w, y), up))
        start(b_share(w, 1, b_unit(w, y), down))
        start(b_share(w, 4, b_unit(w, y), across))

    def b_forward_up(w):
        b_share(w, 0, b_unit(w, ym), up).wait_recv()
        start(b_share(w, 2, left(b_unit(w, ym)), up))
        start(b_share(w, 5, b_unit(w, ym), across))

    def b_forward_down(w):
        b_share(w, 1, b_unit(w, yp), down).wait_recv()
        start(b_share(w, 3, right(b_unit(w, yp)), down))
        start(b_share(w, 6, b_unit(w, yp), across))

    def b_last(w):
        b_share(w, 2, left(b_unit(w, y2)), up).wait_recv()
        b_share(w, 3, right(b_unit(w, y2)), down).wait_recv()
        start(b_share(w, 7, b_unit(w, y2), across))

    def a_relay_up(w):
        rs_up(w, 0, part.at[w, y2 * 2], m1.at[w, 0]).wait_recv()
        relay[w, 0] = (part[w, yp * 2].astype(F32) + m1[w, 0].astype(F32)).astype(BF16)
        start(rs_up(w, 2, relay.at[w, 0], m3.at[w, 0]))

    def a_relay_down(w):
        rs_down(w, 0, part.at[w, y2 * 2 + 1], m1.at[w, 1]).wait_recv()
        relay[w, 1] = (part[w, ym * 2 + 1].astype(F32) + m1[w, 1].astype(F32)).astype(BF16)
        start(rs_down(w, 2, relay.at[w, 1], m3.at[w, 1]))

    def cross(w):
        return remote(xsend.at[w], xrecv.at[w], rs_send.at[w, 3, 0], rs_recv.at[w, 3, 0], across)

    def collect(w):
        rs_up(w, 1, part.at[w, yp * 2 + 1], m2.at[w, 0]).wait_recv()
        rs_down(w, 1, part.at[w, ym * 2], m2.at[w, 1]).wait_recv()
        rs_up(w, 2, relay.at[w, 0], m3.at[w, 0]).wait_recv()
        rs_down(w, 2, relay.at[w, 1], m3.at[w, 1]).wait_recv()
        low = part[w, y * 2].astype(F32) + m3[w, 0].astype(F32) + m2[w, 1].astype(F32)
        high = part[w, y * 2 + 1].astype(F32) + m3[w, 1].astype(F32) + m2[w, 0].astype(F32)
        mine = x == 0
        xsend[w] = jnp.where(mine, high, low).astype(BF16)
        start(cross(w))
        keep[w] = jnp.where(mine, low, high)

    def finish(w):
        cross(w).wait_recv()
        unit = y * 2 + x
        resid[w, unit] = (weight[w] * (keep[w] + xrecv[w].astype(F32))).astype(BF16)
        start(ag(w, 0, unit, across))
        start(ag(w, 1, unit, up))
        start(ag(w, 2, unit, down))

    def share(w):
        unit = y * 2 + 1 - x
        ag(w, 0, unit, across).wait_recv()
        start(ag(w, 3, unit, up))
        start(ag(w, 4, unit, down))

    def forward_up(w):
        ag(w, 1, ym * 2, up).wait_recv()
        start(ag(w, 5, ym * 2, up))

    def forward_down(w):
        ag(w, 1, yp * 2 + 1, down).wait_recv()
        start(ag(w, 6, yp * 2 + 1, down))

    def arrived(w):
        if KINDS[w] == "A":
            for unit in (ym * 2 + 1, yp * 2, y2 * 2, y2 * 2 + 1):
                ag(w, 1, unit, up).wait_recv()
        else:
            for role in range(4, 8):
                b_share(w, role, b_unit(w, y), across).wait_recv()

    def consume(group):
        c0, c1 = group
        lo, hi = c0 * ROWS, c1 * ROWS
        count = hi - lo
        for c in range(c0, c1):
            arrived(c)
        block = resid[c0:c1].reshape(count, NS)
        i_ = lax.broadcasted_iota(jnp.int32, (count, count), 0)
        j_ = lax.broadcasted_iota(jnp.int32, (count, count), 1)
        middle = block[:, lo:hi]
        zero = jnp.zeros_like(middle)
        upper = jnp.where(i_ <= j_, middle, zero)
        lower = jnp.where(i_ > j_, middle, zero)
        if hi < NS:
            upper = jnp.concatenate([upper, block[:, hi:]], axis=1)
        if lo > 0:
            lower = jnp.concatenate([block[:, :lo], lower], axis=1)
        width = g.shape[3]
        step = min(256, width)
        for h in range(2):
            for t in range(width // step):
                cols = slice(t * step, (t + 1) * step)
                zr = dot_nn(upper, g[h, 0, lo:, cols]) - dot_nn(lower, g[h, 1, :hi, cols])
                zi = dot_nn(upper, g[h, 1, lo:, cols]) + dot_nn(lower, g[h, 0, :hi, cols])
                value = g[h, 0, lo:hi, cols].astype(F32) * zr
                value += g[h, 1, lo:hi, cols].astype(F32) * zi
                value = jnp.sum(value, axis=0, keepdims=True)
                if lo > 0:
                    value = value + sens[h, :, cols]
                sens[h, :, cols] = value

    ops = {
        "P": lambda n: produce(GROUPS[n]),
        "C": lambda n: consume(GROUPS[n]),
        "A1u": a_relay_up,
        "A1d": a_relay_down,
        "A2": collect,
        "A3": finish,
        "A4": share,
        "A5u": forward_up,
        "A5d": forward_down,
        "B0": b_sum_far,
        "B1": b_sum_up,
        "B2": b_sum_down,
        "B3": b_sum_own,
        "B4u": b_relay_up,
        "B4d": b_relay_down,
        "B5": b_finish,
        "B6u": b_forward_up,
        "B6d": b_forward_down,
        "B7": b_last,
    }
    for name, n in ORDER:
        ops[name](n)

    f_copies = []
    me = q * 2 + core
    for n, (d, h) in enumerate(peers):
        to_q = lax.rem(q + d, nfreq)
        fsend[n] = basis[core, to_q] * sens[h]
        f_copies.append(remote(fsend.at[n], frecv.at[me], f_send.at[n], f_recv.at[n], peer(d, h)))
        f_copies[-1].start()
    frecv[me] = basis[core, q] * sens[0]
    for copy in f_copies:
        copy.wait_recv()
    total = frecv[0]
    for n in range(1, 2 * nfreq):
        total = total + frecv[n]
    out[...] = total

    for copy in c_copies + swap + sent + f_copies:
        copy.wait_send()


def on_device(green, coeffs, basis, amplitude, block_mask):
    nfreq = lax.axis_size("freq")
    cells = green.shape[3]
    dma = pltpu.SemaphoreType.DMA
    n = 2 * nfreq - 1
    return pl.pallas_call(
        functools.partial(kernel, nfreq),
        out_shape=jax.ShapeDtypeStruct((1, cells), F32),
        in_specs=[pl.BlockSpec(memory_space=pltpu.HBM)] * 5,
        out_specs=pl.BlockSpec(memory_space=pltpu.VMEM),
        scratch_shapes=[
            pltpu.SMEM(basis.shape, F32),
            pltpu.VMEM(amplitude.shape, F32),
            pltpu.SMEM(block_mask.shape, jnp.int32),
            pltpu.VMEM((2, 2, NS, cells), BF16),
            pltpu.VMEM((nfreq, 2, 1, cells), F32),
            pltpu.VMEM((2, 2, 2 * ROWS, cells), BF16),
            pltpu.VMEM((CHUNKS, 8, UNIT, NS), BF16),
            pltpu.VMEM((CHUNKS, 8, UNIT, NS), BF16),
            pltpu.VMEM((CHUNKS, UNIT, NS), F32),
            pltpu.VMEM((CHUNKS, UNIT, NS), F32),
            pltpu.VMEM((CHUNKS, 2, UNIT, NS), BF16),
            pltpu.VMEM((CHUNKS, 2, UNIT, NS), BF16),
            pltpu.VMEM((CHUNKS, 2, UNIT, NS), BF16),
            pltpu.VMEM((CHUNKS, 2, UNIT, NS), BF16),
            pltpu.VMEM((CHUNKS, UNIT, NS), BF16),
            pltpu.VMEM((CHUNKS, UNIT, NS), BF16),
            pltpu.VMEM((CHUNKS, 4, UNIT, NS), BF16),
            pltpu.VMEM((CHUNKS, 3, UNIT, NS), BF16),
            pltpu.VMEM((CHUNKS, 2, UNIT, HALF), BF16),
            pltpu.VMEM((CHUNKS, 2, UNIT, HALF), BF16),
            pltpu.VMEM((CHUNKS, 2, UNIT, HALF), BF16),
            pltpu.VMEM((CHUNKS, 2, UNIT, HALF), F32),
            pltpu.VMEM((CHUNKS, 2, UNIT, HALF), BF16),
            pltpu.VMEM((2, 1, cells), F32),
            pltpu.VMEM((n, 1, cells), F32),
            pltpu.VMEM((2 * nfreq, 1, cells), F32),
            dma((4,)),
            dma((2,)),
            dma((2,)),
            dma((2,)),
            dma((n,)),
            dma((n,)),
            dma((CHUNKS, 4, 2)),
            dma((CHUNKS, 4, 2)),
            dma((CHUNKS, 7)),
            dma((CHUNKS, 8)),
            dma((CHUNKS, 4)),
            dma((CHUNKS, 4)),
            dma((CHUNKS, 3, 2)),
            dma((CHUNKS, 3, 2)),
            dma((CHUNKS, 8)),
            dma((CHUNKS, 8)),
            dma((n,)),
            dma((n,)),
        ],
        compiler_params=pltpu.CompilerParams(
            collective_id=0, has_side_effects=True, vmem_limit_bytes=67043328
        ),
        name="hessian_vector",
    )(green, coeffs, basis, amplitude, block_mask)


def solution(mesh):
    placed = (
        P(None, "freq", None, "cell"),
        P("freq", "cell"),
        P("freq", None),
        P("freq", None),
        P(),
    )
    return jax.shard_map(
        on_device, mesh=mesh, in_specs=placed, out_specs=P("freq", "cell"), check_vma=False
    )
```

```python
import functools

import jax
import jax.numpy as jnp
from jax import lax
from jax.experimental import pallas as pl
from jax.experimental.pallas import tpu as pltpu
from jax.sharding import PartitionSpec as P

MESH = pl.DeviceIdType.MESH
F32, BF16 = jnp.float32, jnp.bfloat16
NS = 1024
ROWS = 128
UNIT = ROWS // 8
HALF = NS // 2
KINDS = "BAABABAB"
GROUPS = ((0, 2), (2, 4), (4, 6), (6, 8))
CHUNKS = len(KINDS)
ORDER = (
    ("P", 0), ("P", 1), ("P", 2), ("B0", 0), ("A1u", 1), ("A1d", 1), ("P", 3), ("B3", 0),
    ("B1", 0), ("B2", 0), ("A1u", 2), ("A1d", 2), ("B0", 3), ("B1", 3), ("A1u", 4), ("A1d", 4),
    ("B2", 3), ("B4u", 0), ("B4d", 0), ("B3", 3), ("A2", 1), ("B0", 5), ("A1u", 6), ("A1d", 6),
    ("B1", 5), ("B2", 5), ("B3", 5), ("A2", 2), ("B4u", 3), ("B4d", 3), ("B0", 7), ("B1", 7),
    ("A2", 4), ("B5", 0), ("B2", 7), ("B4u", 5), ("B4d", 5), ("B3", 7), ("A2", 6), ("A3", 1),
    ("B5", 3), ("B4u", 7), ("B4d", 7), ("A3", 2), ("A3", 4), ("B6u", 0), ("B6d", 0), ("B5", 5),
    ("A3", 6), ("A4", 1), ("B6u", 3), ("B6d", 3), ("B5", 7), ("A4", 2), ("A4", 4), ("B7", 0),
    ("B6u", 5), ("B6d", 5), ("A5u", 1), ("A5d", 1), ("A4", 6), ("B7", 3), ("B6u", 7),
    ("B6d", 7), ("A5u", 2), ("A5d", 2), ("A5u", 4), ("A5d", 4), ("B7", 5), ("C", 0), ("A5u", 6),
    ("A5d", 6), ("B7", 7), ("C", 1), ("C", 2), ("C", 3),
)
BLOCKS = 16
WIDTH = NS // BLOCKS


def dot_nt(a, b):
    return lax.dot_general(a, b, (((1,), (1,)), ((), ())), preferred_element_type=F32)


def dot_nn(a, b):
    return lax.dot_general(a, b, (((1,), (0,)), ((), ())), preferred_element_type=F32)


def kernel(
    nfreq,
    green,
    coeffs,
    basis_in,
    amp_in,
    mask_in,
    out,
    basis,
    amp,
    mask,
    g,
    cbuf,
    sc,
    part,
    resid,
    weight,
    keep,
    m1,
    m2,
    m3,
    relay,
    xsend,
    xrecv,
    bx,
    bsum,
    b1,
    b2,
    b3,
    bhold,
    brelay,
    sens,
    fsend,
    frecv,
    in_sem,
    own_sem,
    swap_send,
    swap_recv,
    c_send,
    c_recv,
    rs_send,
    rs_recv,
    ag_send,
    ag_recv,
    bx_send,
    bx_recv,
    by_send,
    by_recv,
    bg_send,
    bg_recv,
    f_send,
    f_recv,
):
    q = lax.axis_index("freq")
    cell = lax.axis_index("cell")
    core = lax.rem(cell, 2)
    y = lax.rem(lax.div(cell, 2), 4)
    x = lax.div(cell, 8)
    yp, ym, y2 = lax.rem(y + 1, 4), lax.rem(y + 3, 4), lax.rem(y + 2, 4)

    def at(x_, y_, core_):
        return {"freq": q, "cell": x_ * 8 + y_ * 2 + core_}

    up, down = at(x, yp, core), at(x, ym, core)
    across, twin = at(1 - x, y, core), at(x, y, 1 - core)

    far_first = sorted(range(nfreq), key=lambda d: (d % 4 != 2, d % 2 == 0, d == 0))
    peers = [(d, h) for d in far_first for h in (1, 0) if (d, h) != (0, 0)]

    def peer(d, h):
        to_core = core if h == 0 else 1 - core
        to_q = lax.rem(q + d, nfreq)
        return {"freq": to_q, "cell": x * 8 + y * 2 + to_core}

    def remote(src, dst, send, recv, device):
        return pltpu.make_async_remote_copy(
            src_ref=src,
            dst_ref=dst,
            send_sem=send,
            recv_sem=recv,
            device_id=device,
            device_id_type=MESH,
        )

    small = [
        pltpu.make_async_copy(basis_in, basis, in_sem.at[0]),
        pltpu.make_async_copy(amp_in, amp, in_sem.at[1]),
        pltpu.make_async_copy(mask_in, mask, in_sem.at[2]),
        pltpu.make_async_copy(coeffs, cbuf.at[q, 0], in_sem.at[3]),
    ]
    for copy in small:
        copy.start()
    own = [pltpu.make_async_copy(green.at[p, core], g.at[0, p], own_sem.at[p]) for p in range(2)]
    for copy in own:
        copy.start()

    barrier = pltpu.get_barrier_semaphore()
    met = [peer(d, h) for d, h in peers] + [up, down, across]
    for device in met:
        pl.semaphore_signal(barrier, inc=1, device_id=device, device_id_type=MESH)

    small[3].wait()
    pl.semaphore_wait(barrier, len(met))

    c_copies = []
    for n, (d, h) in enumerate(peers):
        c_copies.append(
            remote(cbuf.at[q, 0], cbuf.at[q, h], c_send.at[n], c_recv.at[n], peer(d, h))
        )
        c_copies[-1].start()
    swap = [
        remote(green.at[p, 1 - core], g.at[1, p], swap_send.at[p], swap_recv.at[p], twin)
        for p in range(2)
    ]
    for copy in swap:
        copy.start()

    for copy in small[:3]:
        copy.wait()

    lane = lax.broadcasted_iota(jnp.int32, (1, NS), 1)
    block_of = lane // WIDTH
    amp_row = amp[pl.ds(core, 1), :]
    for w in range(CHUNKS):
        first = w * ROWS + (y * 2 + x) * UNIT
        a = lax.div(first, WIDTH)
        pair = jnp.zeros((1, NS), F32)
        for b in range(BLOCKS):
            m = (mask[a, b] + mask[b, a]).astype(F32)
            pair = pair + jnp.where(block_of == b, m, 0.0)
        row = lax.broadcasted_iota(jnp.int32, (UNIT, NS), 0) + first
        col = lax.broadcasted_iota(jnp.int32, (UNIT, NS), 1)
        same = row == col
        amp_col = jnp.sum(jnp.where(same, amp_row, 0.0), axis=1, keepdims=True)
        weight[w] = jnp.where(same, 0.5, 1.0) * (amp_col * (amp_row * pair))

    for copy in c_copies:
        copy.wait_recv()
    source = []
    for h in range(2):
        total = basis[core, 0] * cbuf[0, h]
        for b in range(1, nfreq):
            total = total + basis[core, b] * cbuf[b, h]
        source.append(total)

    for copy in own:
        copy.wait()

    sent = []

    def start(copy):
        copy.start()
        sent.append(copy)

    def rs_up(w, n, src, dst):
        return remote(src, dst, rs_send.at[w, n, 0], rs_recv.at[w, n, 0], up)

    def rs_down(w, n, src, dst):
        return remote(src, dst, rs_send.at[w, n, 1], rs_recv.at[w, n, 1], down)

    def ag(w, n, unit, device):
        ref = resid.at[w, unit]
        return remote(ref, ref, ag_send.at[w, n], ag_recv.at[w, unit], device)

    def produce(group):
        c0, c1 = group
        lo, hi = c0 * ROWS, c1 * ROWS
        count = hi - lo
        for h in range(2):
            if c0 == 0 and h == 1:
                for copy in swap:
                    copy.wait_recv()
            for p in range(2):
                field = g[h, p, lo:hi, :].astype(F32)
                sc[h, p, :count, :] = (field * source[h]).astype(BF16)

        def real(start, stop):
            total = dot_nt(sc[0, 0, :count], g[0, 0, start:stop])
            total += dot_nt(sc[0, 1, :count], g[0, 1, start:stop])
            total += dot_nt(sc[1, 0, :count], g[1, 0, start:stop])
            total += dot_nt(sc[1, 1, :count], g[1, 1, start:stop])
            return total

        def imag(start, stop):
            plus = dot_nt(sc[0, 1, :count], g[0, 0, start:stop])
            plus += dot_nt(sc[1, 1, :count], g[1, 0, start:stop])
            minus = dot_nt(sc[0, 0, :count], g[0, 1, start:stop])
            minus += dot_nt(sc[1, 0, :count], g[1, 1, start:stop])
            return plus - minus

        def put(start, stop, block):
            shape = (c1 - c0, 8, UNIT, stop - start)
            part[c0:c1, :, :, start:stop] = block.astype(BF16).reshape(shape)

        for start in range(0, lo, 256):
            stop = min(start + 256, lo)
            put(start, stop, imag(start, stop))
        i_ = lax.broadcasted_iota(jnp.int32, (count, count), 0)
        j_ = lax.broadcasted_iota(jnp.int32, (count, count), 1)
        put(lo, hi, jnp.where(i_ <= j_, real(lo, hi), imag(lo, hi)))
        for start in range(hi, NS, 256):
            stop = min(start + 256, NS)
            put(start, stop, real(start, stop))
        for c in range(c0, c1):
            if KINDS[c] == "A":
                start_a(c)
            else:
                start_b(c)

    def start_a(w):
        start(rs_up(w, 0, part.at[w, y2 * 2], m1.at[w, 0]))
        start(rs_down(w, 0, part.at[w, y2 * 2 + 1], m1.at[w, 1]))
        start(rs_up(w, 1, part.at[w, yp * 2 + 1], m2.at[w, 0]))
        start(rs_down(w, 1, part.at[w, ym * 2], m2.at[w, 1]))

    targets = (y2, yp, ym, y)

    def b_cross(w, r):
        src = part.at[w, targets[r] * 2 + 1 - x]
        return remote(src, bx.at[w, r], bx_send.at[w, r], bx_recv.at[w, r], across)

    def b_up(w, n, src, dst):
        return remote(src, dst, by_send.at[w, n, 0], by_recv.at[w, n, 0], up)

    def b_down(w, n, src, dst):
        return remote(src, dst, by_send.at[w, n, 1], by_recv.at[w, n, 1], down)

    def left(ref):
        return ref.at[:, 0:HALF]

    def right(ref):
        return ref.at[:, HALF:NS]

    def b_share(w, role, ref, device):
        return remote(ref, ref, bg_send.at[w, role], bg_recv.at[w, role], device)

    def b_unit(w, t):
        return resid.at[w, t * 2 + x]

    def start_b(w):
        for r in range(4):
            start(b_cross(w, r))

    def b_total(w, r):
        b_cross(w, r).wait_recv()
        return part[w, targets[r] * 2 + x].astype(F32) + bx[w, r].astype(F32)

    def b_sum_far(w):
        bsum[w, 0] = b_total(w, 0).astype(BF16)
        start(b_up(w, 0, left(bsum.at[w, 0]), b1.at[w, 0]))
        start(b_down(w, 0, right(bsum.at[w, 0]), b1.at[w, 1]))

    def b_sum_up(w):
        value = b_total(w, 1)
        bhold[w, 0] = value[:, :HALF]
        bsum[w, 1, :, HALF:] = value[:, HALF:].astype(BF16)
        start(b_up(w, 1, right(bsum.at[w, 1]), b2.at[w, 0]))

    def b_sum_down(w):
        value = b_total(w, 2)
        bhold[w, 1] = value[:, HALF:]
        bsum[w, 2, :, :HALF] = value[:, :HALF].astype(BF16)
        start(b_down(w, 1, left(bsum.at[w, 2]), b2.at[w, 1]))

    def b_sum_own(w):
        keep[w] = b_total(w, 3)

    def b_relay_up(w):
        b_up(w, 0, left(bsum.at[w, 0]), b1.at[w, 0]).wait_recv()
        brelay[w, 0] = (bhold[w, 0] + b1[w, 0].astype(F32)).astype(BF16)
        start(b_up(w, 2, brelay.at[w, 0], b3.at[w, 0]))

    def b_relay_down(w):
        b_down(w, 0, right(bsum.at[w, 0]), b1.at[w, 1]).wait_recv()
        brelay[w, 1] = (bhold[w, 1] + b1[w, 1].astype(F32)).astype(BF16)
        start(b_down(w, 2, brelay.at[w, 1], b3.at[w, 1]))

    def b_finish(w):
        b_up(w, 1, right(bsum.at[w, 1]), b2.at[w, 0]).wait_recv()
        b_down(w, 1, left(bsum.at[w, 2]), b2.at[w, 1]).wait_recv()
        b_up(w, 2, brelay.at[w, 0], b3.at[w, 0]).wait_recv()
        b_down(w, 2, brelay.at[w, 1], b3.at[w, 1]).wait_recv()
        low = keep[w, :, :HALF] + b3[w, 0].astype(F32) + b2[w, 1].astype(F32)
        high = keep[w, :, HALF:] + b3[w, 1].astype(F32) + b2[w, 0].astype(F32)
        unit = y * 2 + x
        resid[w, unit, :, :HALF] = (weight[w, :, :HALF] * low).astype(BF16)
        resid[w, unit, :, HALF:] = (weight[w, :, HALF:] * high).astype(BF16)
        start(b_share(w, 0, b_unit(w, y), up))
        start(b_share(w, 1, b_unit(w, y), down))
        start(b_share(w, 4, b_unit(w, y), across))

    def b_forward_up(w):
        b_share(w, 0, b_unit(w, ym), up).wait_recv()
        start(b_share(w, 2, left(b_unit(w, ym)), up))
        start(b_share(w, 5, b_unit(w, ym), across))

    def b_forward_down(w):
        b_share(w, 1, b_unit(w, yp), down).wait_recv()
        start(b_share(w, 3, right(b_unit(w, yp)), down))
        start(b_share(w, 6, b_unit(w, yp), across))

    def b_last(w):
        b_share(w, 2, left(b_unit(w, y2)), up).wait_recv()
        b_share(w, 3, right(b_unit(w, y2)), down).wait_recv()
        start(b_share(w, 7, b_unit(w, y2), across))

    def a_relay_up(w):
        rs_up(w, 0, part.at[w, y2 * 2], m1.at[w, 0]).wait_recv()
        relay[w, 0] = (part[w, yp * 2].astype(F32) + m1[w, 0].astype(F32)).astype(BF16)
        start(rs_up(w, 2, relay.at[w, 0], m3.at[w, 0]))

    def a_relay_down(w):
        rs_down(w, 0, part.at[w, y2 * 2 + 1], m1.at[w, 1]).wait_recv()
        relay[w, 1] = (part[w, ym * 2 + 1].astype(F32) + m1[w, 1].astype(F32)).astype(BF16)
        start(rs_down(w, 2, relay.at[w, 1], m3.at[w, 1]))

    def cross(w):
        return remote(xsend.at[w], xrecv.at[w], rs_send.at[w, 3, 0], rs_recv.at[w, 3, 0], across)

    def collect(w):
        rs_up(w, 1, part.at[w, yp * 2 + 1], m2.at[w, 0]).wait_recv()
        rs_down(w, 1, part.at[w, ym * 2], m2.at[w, 1]).wait_recv()
        rs_up(w, 2, relay.at[w, 0], m3.at[w, 0]).wait_recv()
        rs_down(w, 2, relay.at[w, 1], m3.at[w, 1]).wait_recv()
        low = part[w, y * 2].astype(F32) + m3[w, 0].astype(F32) + m2[w, 1].astype(F32)
        high = part[w, y * 2 + 1].astype(F32) + m3[w, 1].astype(F32) + m2[w, 0].astype(F32)
        mine = x == 0
        xsend[w] = jnp.where(mine, high, low).astype(BF16)
        start(cross(w))
        keep[w] = jnp.where(mine, low, high)

    def finish(w):
        cross(w).wait_recv()
        unit = y * 2 + x
        resid[w, unit] = (weight[w] * (keep[w] + xrecv[w].astype(F32))).astype(BF16)
        start(ag(w, 0, unit, across))
        start(ag(w, 1, unit, up))
        start(ag(w, 2, unit, down))

    def share(w):
        unit = y * 2 + 1 - x
        ag(w, 0, unit, across).wait_recv()
        start(ag(w, 3, unit, up))
        start(ag(w, 4, unit, down))

    def forward_up(w):
        ag(w, 1, ym * 2, up).wait_recv()
        start(ag(w, 5, ym * 2, up))

    def forward_down(w):
        ag(w, 1, yp * 2 + 1, down).wait_recv()
        start(ag(w, 6, yp * 2 + 1, down))

    def arrived(w):
        if KINDS[w] == "A":
            for unit in (ym * 2 + 1, yp * 2, y2 * 2, y2 * 2 + 1):
                ag(w, 1, unit, up).wait_recv()
        else:
            for role in range(4, 8):
                b_share(w, role, b_unit(w, y), across).wait_recv()

    def consume(group):
        c0, c1 = group
        lo, hi = c0 * ROWS, c1 * ROWS
        count = hi - lo
        for c in range(c0, c1):
            arrived(c)
        block = resid[c0:c1].reshape(count, NS)
        i_ = lax.broadcasted_iota(jnp.int32, (count, count), 0)
        j_ = lax.broadcasted_iota(jnp.int32, (count, count), 1)
        middle = block[:, lo:hi]
        zero = jnp.zeros_like(middle)
        upper = jnp.where(i_ <= j_, middle, zero)
        lower = jnp.where(i_ > j_, middle, zero)
        if hi < NS:
            upper = jnp.concatenate([upper, block[:, hi:]], axis=1)
        if lo > 0:
            lower = jnp.concatenate([block[:, :lo], lower], axis=1)
        width = g.shape[3]
        step = min(256, width)
        for h in range(2):
            for t in range(width // step):
                cols = slice(t * step, (t + 1) * step)
                zr = dot_nn(upper, g[h, 0, lo:, cols]) - dot_nn(lower, g[h, 1, :hi, cols])
                zi = dot_nn(upper, g[h, 1, lo:, cols]) + dot_nn(lower, g[h, 0, :hi, cols])
                value = g[h, 0, lo:hi, cols].astype(F32) * zr
                value += g[h, 1, lo:hi, cols].astype(F32) * zi
                value = jnp.sum(value, axis=0, keepdims=True)
                if lo > 0:
                    value = value + sens[h, :, cols]
                sens[h, :, cols] = value

    ops = {
        "P": lambda n: produce(GROUPS[n]),
        "C": lambda n: consume(GROUPS[n]),
        "A1u": a_relay_up,
        "A1d": a_relay_down,
        "A2": collect,
        "A3": finish,
        "A4": share,
        "A5u": forward_up,
        "A5d": forward_down,
        "B0": b_sum_far,
        "B1": b_sum_up,
        "B2": b_sum_down,
        "B3": b_sum_own,
        "B4u": b_relay_up,
        "B4d": b_relay_down,
        "B5": b_finish,
        "B6u": b_forward_up,
        "B6d": b_forward_down,
        "B7": b_last,
    }
    for name, n in ORDER:
        ops[name](n)

    f_copies = []
    me = q * 2 + core
    for n, (d, h) in enumerate(peers):
        to_q = lax.rem(q + d, nfreq)
        fsend[n] = basis[core, to_q] * sens[h]
        f_copies.append(remote(fsend.at[n], frecv.at[me], f_send.at[n], f_recv.at[n], peer(d, h)))
        f_copies[-1].start()
    frecv[me] = basis[core, q] * sens[0]
    for copy in f_copies:
        copy.wait_recv()
    total = frecv[0]
    for n in range(1, 2 * nfreq):
        total = total + frecv[n]
    out[...] = total

    for copy in c_copies + swap + sent + f_copies:
        copy.wait_send()


def on_device(green, coeffs, basis, amplitude, block_mask):
    nfreq = lax.axis_size("freq")
    cells = green.shape[3]
    dma = pltpu.SemaphoreType.DMA
    n = 2 * nfreq - 1
    return pl.pallas_call(
        functools.partial(kernel, nfreq),
        out_shape=jax.ShapeDtypeStruct((1, cells), F32),
        in_specs=[pl.BlockSpec(memory_space=pltpu.HBM)] * 5,
        out_specs=pl.BlockSpec(memory_space=pltpu.VMEM),
        scratch_shapes=[
            pltpu.SMEM(basis.shape, F32),
            pltpu.VMEM(amplitude.shape, F32),
            pltpu.SMEM(block_mask.shape, jnp.int32),
            pltpu.VMEM((2, 2, NS, cells), BF16),
            pltpu.VMEM((nfreq, 2, 1, cells), F32),
            pltpu.VMEM((2, 2, 2 * ROWS, cells), BF16),
            pltpu.VMEM((CHUNKS, 8, UNIT, NS), BF16),
            pltpu.VMEM((CHUNKS, 8, UNIT, NS), BF16),
            pltpu.VMEM((CHUNKS, UNIT, NS), F32),
            pltpu.VMEM((CHUNKS, UNIT, NS), F32),
            pltpu.VMEM((CHUNKS, 2, UNIT, NS), BF16),
            pltpu.VMEM((CHUNKS, 2, UNIT, NS), BF16),
            pltpu.VMEM((CHUNKS, 2, UNIT, NS), BF16),
            pltpu.VMEM((CHUNKS, 2, UNIT, NS), BF16),
            pltpu.VMEM((CHUNKS, UNIT, NS), BF16),
            pltpu.VMEM((CHUNKS, UNIT, NS), BF16),
            pltpu.VMEM((CHUNKS, 4, UNIT, NS), BF16),
            pltpu.VMEM((CHUNKS, 3, UNIT, NS), BF16),
            pltpu.VMEM((CHUNKS, 2, UNIT, HALF), BF16),
            pltpu.VMEM((CHUNKS, 2, UNIT, HALF), BF16),
            pltpu.VMEM((CHUNKS, 2, UNIT, HALF), BF16),
            pltpu.VMEM((CHUNKS, 2, UNIT, HALF), F32),
            pltpu.VMEM((CHUNKS, 2, UNIT, HALF), BF16),
            pltpu.VMEM((2, 1, cells), F32),
            pltpu.VMEM((n, 1, cells), F32),
            pltpu.VMEM((2 * nfreq, 1, cells), F32),
            dma((4,)),
            dma((2,)),
            dma((2,)),
            dma((2,)),
            dma((n,)),
            dma((n,)),
            dma((CHUNKS, 4, 2)),
            dma((CHUNKS, 4, 2)),
            dma((CHUNKS, 7)),
            dma((CHUNKS, 8)),
            dma((CHUNKS, 4)),
            dma((CHUNKS, 4)),
            dma((CHUNKS, 3, 2)),
            dma((CHUNKS, 3, 2)),
            dma((CHUNKS, 8)),
            dma((CHUNKS, 8)),
            dma((n,)),
            dma((n,)),
        ],
        compiler_params=pltpu.CompilerParams(
            collective_id=0, has_side_effects=True, vmem_limit_bytes=67043328
        ),
        name="hessian_vector",
    )(green, coeffs, basis, amplitude, block_mask)


def solution(mesh):
    placed = (
        P(None, "freq", None, "cell"),
        P("freq", "cell"),
        P("freq", None),
        P("freq", None),
        P(),
    )
    return jax.shard_map(
        on_device, mesh=mesh, in_specs=placed, out_specs=P("freq", "cell"), check_vma=False
    )
```
